32 devices in a mesh: cube: 2 (over y), facet: 4 (over z), chan: 2 (over x), sub: 2 (over core).
Axes of the slice: x: 2, y: 2, z: 4, core: 2. Of those that a mesh axis runs over, the one named last changes fastest.
Arguments:
- image: float32 [128, 256, 512], P(('cube', 'chan'), ('facet', 'sub')), parts along dimension 0, may hold values from 0 to 2
- dual_nuclear: float32 [128, 256, 512], P(('cube', 'chan'), ('facet', 'sub')), parts along dimension 0, may hold values from -25 to 25
- dual_wavelet: bfloat16 [128, 4, 256, 512], P(('cube', 'chan'), None, ('facet', 'sub')), parts along dimension 0, may hold values from -3 to 3
- dual_data: float32 [128, 2, 512, 128], P(('cube', 'chan'), None, ('facet', 'sub')), parts along dimension 0, may hold values from -3 to 3
- observed: float32 [128, 2, 512, 128], P(('cube', 'chan'), None, ('facet', 'sub')), parts along dimension 0, may hold values from -6 to 6
- sample_rows: int32 [128, 128], P(('cube', 'chan')), parts along dimension 0, may hold values from 0 to 255
Outputs:
- image_next: float32 [128, 256, 512], P(('cube', 'chan'), ('facet', 'sub')), parts along dimension 0
- nuclear_next: float32 [128, 256, 512], P(('cube', 'chan'), ('facet', 'sub')), parts along dimension 0
- wavelet_next: bfloat16 [128, 4, 256, 512], P(('cube', 'chan'), None, ('facet', 'sub')), parts along dimension 0
- data_next: float32 [128, 2, 512, 128], P(('cube', 'chan'), None, ('facet', 'sub')), parts along dimension 0
The draws below stay inside these ranges and needn't reach their ends.
There are 2 independent parts, one for each index of `cube`. The reference program is written for one: setup_inputs(seed, part) draws one part's arguments, and reference() takes and returns one part's arrays. A program takes and returns all parts, laid end to end along the dimension named above; each array names one. Nothing has to cross between parts.
Inputs may be any that keep to these rules, and one draw needn't show every extreme that they name: `sample_rows`: indices may repeat within a channel.
All inputs are finite; a program needn't handle non-finite values.
Results may differ from the reference program's by a relative error of at most 0.0083.
Values may be sent and summed in bfloat16 or wider, within the bound.
A program may use at most 128 MiB of HBM per device.

```python
import math
import jax
import jax.numpy as jnp
from jax import lax

CH = 64
NX = 512
SAMPLES = 128
NS_STEPS = 6
NY = 256
FACET_PIX = 32768
N_FACET = 4


def draw_dual_nuclear(key, part):
    key_scale, key_noise = jax.random.split(key, 2)
    scales = jnp.exp(jax.random.uniform(key_scale, (CH, 1, 1), jnp.float32, 0.0, jnp.log(10.0)))
    noise = jnp.clip(jax.random.normal(key_noise, (CH, NY, NX), jnp.float32), -4.0, 4.0)
    result = 0.3 * scales * noise
    return result


def plant(entries, own_key, smallest, high):
    place = [jax.random.randint(jax.random.fold_in(own_key, axis), (), 0, length) for axis, length in enumerate(entries.shape)]
    widest = entries.shape.index(max(entries.shape))
    next_to = place[:widest] + [(place[widest] + 1) % entries.shape[widest]] + place[widest + 1:]
    return entries.at[tuple(place)].set(smallest).at[tuple(next_to)].set(high)


def steps_of(stream_key, dims, cuts, low, high):
    def one(axis_at, shards_of):
        heights = jax.random.uniform(jax.random.fold_in(jax.random.fold_in(stream_key, 6), axis_at), (shards_of,), jnp.float32, low / len(cuts), high / len(cuts))
        return jnp.repeat(jnp.exp(heights), dims[axis_at] // shards_of).reshape((-1,) + (1,) * (len(dims) - axis_at - 1))

    factor_of = one(*cuts[0])
    for cut in cuts[1:]:
        factor_of = factor_of * one(*cut)
    return factor_of


def scatter_about(own_key, shape, spread, most, cuts=(), kind=jnp.bfloat16):
    drawn = spread * jax.random.normal(own_key, shape, jnp.float32)
    if cuts:
        drawn = drawn * steps_of(own_key, shape, cuts, -0.22, 0.18)
    return jnp.clip(drawn, -most, most).astype(kind)


def setup_inputs(seed: int = 0, part: int = 0) -> dict:
    streams_of = jax.random.split(jax.random.key(seed), 7)
    part_splits = jax.random.split(jax.random.fold_in(streams_of[6], part), 7)
    image = jnp.clip(2.0 * jax.random.uniform(part_splits[0], (CH, NY, NX), jnp.float32) ** steps_of(part_splits[0], (CH, NY, NX), ((0, 2), (1, 8)), -0.2, 0.2), 0.0, 2.0)
    dual_nuclear = draw_dual_nuclear(jax.random.fold_in(jax.random.fold_in(streams_of[6], part), 71), part)
    dual_wavelet = scatter_about(part_splits[2], (CH, 4, NY, NX), 0.5, 3.0, ((0, 2), (2, 8)))
    dual_data = scatter_about(part_splits[3], (CH, 2, NX, SAMPLES), 0.5, 3.0, ((0, 2), (2, 8)), jnp.float32)
    observed = scatter_about(part_splits[4], (CH, 2, NX, SAMPLES), 1.0, 6.0, ((0, 2), (2, 8)), jnp.float32)
    sample_rows = plant(jax.random.randint(part_splits[5], (CH, SAMPLES), 0, NY), jax.random.fold_in(part_splits[5], 1), 0, NY - 1).astype(jnp.int32)
    return {"image": image, "dual_nuclear": dual_nuclear, "dual_wavelet": dual_wavelet, "dual_data": dual_data, "observed": observed, "sample_rows": sample_rows}


LOWPASS = [0.48296291314453416, 0.8365163037378079, 0.2241438680420134, -0.12940952255126037]
FILTERS = [[value / math.sqrt(2.0) for value in LOWPASS], [(-1.0) ** index * LOWPASS[3 - index] / math.sqrt(2.0) for index in range(4)]]
HIGH = lax.Precision.HIGHEST

def filter_last(values, taps, adjoint):
    length = values.shape[-1]
    widths = [(0, 0)] * (values.ndim - 1) + [(2, 1) if adjoint else (1, 2)]
    padded = jnp.pad(values, widths)
    if adjoint:
        return sum((taps[index] * padded[..., 3 - index:3 - index + length] for index in range(4)))
    return sum((taps[index] * padded[..., index:index + length] for index in range(4)))

def filter_rows(values, taps, adjoint):
    return jnp.swapaxes(filter_last(jnp.swapaxes(values, -1, -2), taps, adjoint), -1, -2)

def analysis(field):
    bands = []
    for row_band in range(2):
        rowed = filter_rows(field, FILTERS[row_band], False)
        for col_band in range(2):
            bands.append(filter_last(rowed, FILTERS[col_band], False))
    return jnp.stack(bands, 1)

def synthesis(bands):
    total = 0.0
    for row_band in range(2):
        colled = sum((filter_last(bands[:, 2 * row_band + col_band], FILTERS[col_band], True) for col_band in range(2)))
        total = total + filter_rows(colled, FILTERS[row_band], True)
    return total

def lowered(values):
    return lax.optimization_barrier(values.astype(jnp.bfloat16)).astype(jnp.float32)

def phase_tables(freqs, places, period):
    product = freqs.astype(jnp.int32)[..., None] * places.astype(jnp.int32) % period
    angles = 2.0 * math.pi / period * product.astype(jnp.float32)
    norm = 1.0 / math.sqrt(period)
    return (lowered(jnp.cos(angles) * norm), lowered(jnp.sin(angles) * norm))

def reference(image, dual_nuclear, dual_wavelet, dual_data, observed, sample_rows):
    col_places = jnp.arange(NX, dtype=jnp.int32)
    row_places = jnp.arange(NY, dtype=jnp.int32)
    col_cos, col_sin = phase_tables(col_places, col_places, NX)
    row_cos, row_sin = phase_tables(sample_rows, row_places, NY)
    dual_real = lowered(dual_data[:, 0])
    dual_imag = lowered(dual_data[:, 1])
    spread_real = jnp.einsum('cky,cqk->cyq', row_cos, dual_real, precision=HIGH) - jnp.einsum('cky,cqk->cyq', row_sin, dual_imag, precision=HIGH)
    spread_imag = jnp.einsum('cky,cqk->cyq', row_cos, dual_imag, precision=HIGH) + jnp.einsum('cky,cqk->cyq', row_sin, dual_real, precision=HIGH)
    spread_real = lowered(spread_real)
    spread_imag = lowered(spread_imag)
    back_data = jnp.einsum('cyq,qx->cyx', spread_real, col_cos, precision=HIGH) - jnp.einsum('cyq,qx->cyx', spread_imag, col_sin, precision=HIGH)
    wave_float = dual_wavelet.astype(jnp.float32)
    back = back_data + synthesis(wave_float)
    image_next = jnp.maximum(image - 0.5 * (back + dual_nuclear), 0.0)
    field = 2.0 * image_next - image
    field_low = lowered(field)
    spec_real = lowered(jnp.einsum('cyx,xq->cyq', field_low, col_cos, precision=HIGH))
    spec_imag = lowered(-jnp.einsum('cyx,xq->cyq', field_low, col_sin, precision=HIGH))
    samp_real = jnp.einsum('cky,cyq->cqk', row_cos, spec_real, precision=HIGH) + jnp.einsum('cky,cyq->cqk', row_sin, spec_imag, precision=HIGH)
    samp_imag = jnp.einsum('cky,cyq->cqk', row_cos, spec_imag, precision=HIGH) - jnp.einsum('cky,cyq->cqk', row_sin, spec_real, precision=HIGH)
    sampled = jnp.stack([samp_real, samp_imag], 1)
    data_next = (dual_data + 0.5 * (sampled - observed)) / 1.5
    bands = wave_float + 0.5 * analysis(field)
    power = lax.optimization_barrier(jnp.sum(bands * bands, 0))
    limit = 0.6 * math.sqrt(CH)
    wavelet_next = (bands / jnp.maximum(1.0, jnp.sqrt(power) / limit)).astype(jnp.bfloat16)
    stacked = (dual_nuclear + field).astype(jnp.bfloat16)
    facets = stacked.reshape(CH, N_FACET, -1).transpose(1, 0, 2).astype(jnp.float32)
    gram = jnp.einsum('fcp,fdp->fcd', facets, facets, precision=HIGH)
    trace_sum = jnp.trace(gram, axis1=1, axis2=2)
    approx = (2.0 / trace_sum)[:, None, None] * gram
    eye_mat = jnp.broadcast_to(jnp.eye(CH, dtype=jnp.float32), gram.shape)
    root = eye_mat
    for turn in range(NS_STEPS):
        newton = 1.5 * eye_mat - 0.5 * jnp.einsum('fij,fjk->fik', root, approx, precision=HIGH)
        approx = jnp.einsum('fij,fjk->fik', approx, newton, precision=HIGH)
        root = jnp.einsum('fij,fjk->fik', newton, root, precision=HIGH)
    root_low = lowered(root)
    mixed = jnp.einsum('fcd,fdp->fcp', root_low, facets, precision=HIGH)
    mixed = mixed * jnp.sqrt(2.0 * FACET_PIX / trace_sum)[:, None, None]
    nuclear_next = mixed.transpose(1, 0, 2).reshape(CH, NY, NX)
    return (image_next, nuclear_next, wavelet_next, data_next)
```

```python
import functools
import math

import jax
import jax.numpy as jnp
import numpy as np
from jax import lax
from jax.experimental import pallas as pl
from jax.experimental.pallas import tpu as pltpu
from jax.sharding import PartitionSpec as P

CH = 64
NS_STEPS = 6


LOWPASS = [0.48296291314453416, 0.8365163037378079, 0.2241438680420134, -0.12940952255126037]
FILTERS = [
    [value / math.sqrt(2.0) for value in LOWPASS],
    [(-1.0) ** index * LOWPASS[3 - index] / math.sqrt(2.0) for index in range(4)],
]
HIGH = lax.Precision.HIGHEST
LOW = jnp.bfloat16
MESH = pl.DeviceIdType.MESH
FULL = jnp.float32


def phase_base(period):
    places = np.arange(period)
    angles = np.float32(2.0 * math.pi / period) * (np.outer(places, places) % period).astype(np.float32)
    norm = np.float32(1.0 / math.sqrt(period))
    return np.cos(angles) * norm, np.sin(angles) * norm


def row_base(height):
    return jnp.asarray(np.concatenate(phase_base(height), 0).astype(LOW))


def col_base(columns, parts):
    cosine, sine = (t.reshape(parts, columns // parts, columns) for t in phase_base(columns))
    return jnp.asarray(np.concatenate([cosine, -sine], 1).astype(LOW))


def sample_tables(rows, base):
    height, samples = base.shape[1], rows.shape[1]
    hot = lax.broadcasted_iota(jnp.int32, (height, samples), 0) == rows
    hot = jnp.where(hot, 1.0, 0.0).astype(LOW)
    return jnp.dot(base, hot, preferred_element_type=jnp.float32).astype(LOW)


def contract(left, right, left_dim, right_dim):
    return lax.dot_general(
        left, right, (((left_dim,), (right_dim,)), ((), ())), preferred_element_type=jnp.float32
    )


def shifted(values, offset, axis):
    length = values.shape[axis]
    if offset == 0:
        return values
    place = lax.broadcasted_iota(jnp.int32, values.shape, axis) + offset
    moved = pltpu.roll(values, (-offset) % length, axis)
    return jnp.where((place >= 0) & (place < length), moved, 0.0)


def chunk_sizes(channels):
    unit = math.gcd(channels, 4)
    sizes, left = [unit], channels - 2 * unit
    while left > 0:
        sizes.append(min(left, 2 * unit))
        left -= sizes[-1]
    return sizes + [unit] * (left == 0)


def step_kernel(
    facets, halves, chans, sizes,
    rows_hbm, image_hbm, nuclear_hbm, wave_hbm, dual_hbm, obs_hbm, base_hbm, cols_hbm,
    next_ref, mixed_ref, wavelet_ref, data_ref,
    rows_ref, obs_ref, base_ref, cols_ref, load_sem,
    send_back, recv_back, send_spec, recv_spec, synth, field_ref, flat_ref, lane_ref, bands_ref,
    stack_ref, power_ref, powers_ref, scale_ref, gram_ref, root_ref, up_ref, down_ref,
    edge_up, edge_up_in, edge_down, edge_down_in, rim_up, rim_up_in, rim_down, rim_down_in,
    piece_send, piece_recv, edge_send, edge_recv, stack_send, stack_recv,
    power_send, power_recv, gram_send, gram_recv,
):
    parts = facets * halves
    channels, own, columns = next_ref.shape
    height = base_ref.shape[1]
    lanes = send_back.shape[3]
    tiles = columns // 128
    width = lanes // 2
    chunks = len(sizes)
    firsts = [sum(sizes[:i]) for i in range(chunks)]
    half = lax.axis_index("sub")
    me = lax.axis_index("facet") * halves + half
    chan = lax.axis_index("chan")

    def place(peer):
        return {"facet": lax.div(peer, halves), "sub": lax.rem(peer, halves)}

    def remote(source, target, sent, received, device):
        return pltpu.make_async_remote_copy(
            src_ref=source, dst_ref=target, send_sem=sent, recv_sem=received,
            device_id=device, device_id_type=MESH,
        )

    def piece_copy(phase, chunk, d):
        source, target = ((send_back, recv_back), (send_spec, recv_spec))[phase]
        peer = lax.rem(me + d, parts)
        span = pl.ds(firsts[chunk], sizes[chunk])
        return remote(
            source.at[peer, span], target.at[me, span],
            piece_send.at[phase, chunk, d - 1], piece_recv.at[phase, chunk, d - 1], place(peer),
        )

    def chan_copy(buffer, sent, received, d):
        return remote(
            buffer.at[chan], buffer.at[chan], sent.at[d - 1], received.at[d - 1],
            {"chan": lax.rem(chan + d, chans)},
        )

    def gram_copy(d):
        return remote(
            gram_ref.at[half], gram_ref.at[half], gram_send.at[d - 1], gram_recv.at[d - 1],
            {"sub": lax.rem(half + d, halves)},
        )

    def each(low, high, action):
        def run(i, carry):
            action(i)
            return carry

        lax.fori_loop(low, high, run, 0)

    def rim_copy(slot, source, target, up):
        peer = lax.rem(me + (parts - 1 if up else 1), parts)
        return remote(source, target, edge_send.at[slot], edge_recv.at[slot], place(peer))

    def neighbours(slot, up_source, up_target, down_source, down_target, action):
        @pl.when(me > 0)
        def _():
            action(rim_copy(slot, up_source, up_target, True), True)

        @pl.when(me < parts - 1)
        def _():
            action(rim_copy(slot + 1, down_source, down_target, False), False)

    def started(copy, up):
        copy.start()

    def arrived(slot, up_source, up_target, down_source, down_target):
        @pl.when(me < parts - 1)
        def _():
            rim_copy(slot, up_source, up_target, True).wait_recv()

        @pl.when(me > 0)
        def _():
            rim_copy(slot + 1, down_source, down_target, False).wait_recv()

    def left(copy, up):
        copy.wait_send()

    early, late = pl.ds(0, sizes[0]), pl.ds(sizes[0], channels - sizes[0])
    loads = [
        pltpu.make_async_copy(source, target, load_sem.at[i])
        for i, (source, target) in enumerate(
            (
                (base_hbm, base_ref), (rows_hbm, rows_ref),
                (dual_hbm.at[early], data_ref.at[early]), (dual_hbm.at[late], data_ref.at[late]),
                (wave_hbm, wavelet_ref), (image_hbm, next_ref), (nuclear_hbm, mixed_ref),
                (cols_hbm, cols_ref), (obs_hbm, obs_ref),
            )
        )
    ]
    for load in loads:
        load.start()

    for buffer in (edge_up_in, edge_down_in, rim_up_in, rim_down_in):
        buffer[...] = jnp.zeros_like(buffer)

    barrier = pltpu.get_barrier_semaphore()
    each(
        1, parts,
        lambda d: pl.semaphore_signal(
            barrier, inc=1, device_id=place(lax.rem(me + d, parts)), device_id_type=MESH
        ),
    )
    each(
        1, chans,
        lambda d: pl.semaphore_signal(
            barrier, inc=1, device_id={"chan": lax.rem(chan + d, chans)}, device_id_type=MESH
        ),
    )

    def spread(c):
        tables = sample_tables(rows_ref[c], base_ref[...])
        real = data_ref[c, 0].astype(LOW)
        imag = data_ref[c, 1].astype(LOW)
        total = contract(tables[:height], jnp.concatenate([real, imag], 0), 1, 1)
        total += contract(tables[height:], jnp.concatenate([-imag, real], 0), 1, 1)
        send_back[:, c] = total.astype(LOW).reshape(parts, own, lanes)

    def by_group(chunk, action):
        pair = math.gcd(sizes[chunk], 4)

        def run(g):
            for i in range(pair):
                action(firsts[chunk] + g * pair + i)

        each(0, sizes[chunk] // pair, run)

    def send_pieces(phase, chunk):
        each(1, parts, lambda d: piece_copy(phase, chunk, d).start())

    def wave(c):
        colled = []
        for row_band in range(2):
            first = wavelet_ref[c, 2 * row_band].astype(FULL)
            second = wavelet_ref[c, 2 * row_band + 1].astype(FULL)
            colled.append(
                sum(
                    shifted(FILTERS[0][k] * first + FILTERS[1][k] * second, 1 - k, 1)
                    for k in range(4)
                )
            )
        tapped = [FILTERS[0][k] * colled[0] + FILTERS[1][k] * colled[1] for k in range(4)]
        synth[c] = sum(shifted(tapped[k], 1 - k, 0) for k in range(4))
        up_ref[0, pl.ds(c, 1), :] = tapped[0][0:1]
        below = tapped[2] + pltpu.roll(tapped[3], 1, 0)
        down_ref[0, pl.ds(c, 1), :] = below[own - 1 : own]
        down_ref[1, pl.ds(c, 1), :] = tapped[3][own - 1 : own]

    edges = (0, edge_up, edge_up_in, edge_down, edge_down_in)
    for load in loads[:3]:
        load.wait()
    for chunk in range(chunks):
        if chunk == 1:
            loads[3].wait()
        by_group(chunk, spread)
        if chunk == 0:
            pl.semaphore_wait(barrier, parts + chans - 2)
        send_pieces(0, chunk)
        if chunk == min(1, chunks - 1):
            loads[4].wait()
            each(0, channels, wave)
            edge_up[...] = up_ref[0].astype(LOW)
            edge_down[...] = down_ref[...].astype(LOW)
            neighbours(*edges, started)
    each(0, channels, lambda c: recv_back.__setitem__((me, c), send_back[me, c]))

    for load in loads[5:8]:
        load.wait()
    arrived(*edges)
    up_ref[0] = edge_up_in[...].astype(FULL)
    down_ref[...] = edge_down_in[...].astype(FULL)
    row = lax.broadcasted_iota(jnp.int32, (own, columns), 0)
    group = 2 if lanes == 128 and parts % 2 == 0 else 1

    for chunk in range(chunks):
        each(1, parts, lambda d: piece_copy(0, chunk, d).wait_recv())
        first, block = firsts[chunk], sizes[chunk]
        span = pl.ds(first, block)
        back = 0.0
        for p in range(0, parts, group):
            pieces = [recv_back[p + i, span].reshape(block * own, lanes) for i in range(group)]
            base = cols_ref[p : p + group].reshape(group * lanes, columns)
            back = back + contract(jnp.concatenate(pieces, 1), base, 1, 0)
        flat_ref[pl.ds(first * own, block * own), :] = back

        def update(c):
            start = pl.multiple_of(c * own, own)
            total = flat_ref[pl.ds(start, own), :] + synth[c]
            total += jnp.where(row == own - 1, up_ref[0, pl.ds(c, 1), :], 0.0)
            total += jnp.where(row == 0, down_ref[0, pl.ds(c, 1), :], 0.0)
            total += jnp.where(row == 1, down_ref[1, pl.ds(c, 1), :], 0.0)
            image = next_ref[c]
            nuclear = mixed_ref[c]
            image_next = jnp.maximum(image - 0.5 * (total + nuclear), 0.0)
            field = 2.0 * image_next - image
            next_ref[c] = image_next
            field_ref[c] = field
            stacked = nuclear + field
            for j in range(tiles):
                lane_ref[j, pl.ds(start, own), :] = stacked[:, j * 128 : (j + 1) * 128]
            up_ref[0, pl.ds(c, 1), :] = field[0:1]
            up_ref[1, pl.ds(c, 1), :] = field[1:2]
            down_ref[0, pl.ds(c, 1), :] = field[own - 1 : own]

        each(first, first + block, update)
        low = field_ref[span].reshape(block * own, columns).astype(LOW)
        for p in range(0, parts, group):
            base = cols_ref[p : p + group].reshape(group * lanes, columns)
            spec = contract(low, base, 1, 1).astype(LOW)
            for i in range(group):
                send_spec[p + i, span] = spec[:, i * lanes : (i + 1) * lanes].reshape(
                    block, own, lanes
                )
        if chunk == 0:
            send_pieces(1, chunk)

    rims = (2, rim_up, rim_up_in, rim_down, rim_down_in)
    rim_up[...] = up_ref[...].astype(LOW)
    rim_down[...] = down_ref[0].astype(LOW)
    neighbours(*rims, started)
    for chunk in range(1, chunks):
        send_pieces(1, chunk)

    for r in range(own):
        for j in range(tiles):
            picked = lane_ref[j, pl.ds(r, channels, stride=own), :]
            stack_ref[chan, r, :, j * 128 : (j + 1) * 128] = picked.astype(LOW)
    each(1, chans, lambda d: chan_copy(stack_ref, stack_send, stack_recv, d).start())
    each(0, channels, lambda c: recv_spec.__setitem__((me, c), send_spec[me, c]))
    power_ref[...] = jnp.zeros_like(power_ref)
    arrived(*rims)
    up_ref[...] = rim_up_in[...].astype(FULL)
    down_ref[0] = rim_down_in[...].astype(FULL)

    def analyse(c):
        field = field_ref[c]
        above = down_ref[0, pl.ds(c, 1), :]
        below = up_ref[0, pl.ds(c, 1), :]
        beyond = up_ref[1, pl.ds(c, 1), :]
        moved = [
            jnp.where(row == 0, above, pltpu.roll(field, 1, 0)),
            field,
            jnp.where(row == own - 1, below, pltpu.roll(field, own - 1, 0)),
            jnp.where(
                row == own - 1, beyond,
                jnp.where(row == own - 2, below, pltpu.roll(field, own - 2, 0)),
            ),
        ]
        for row_band in range(2):
            rowed = sum(FILTERS[row_band][k] * moved[k] for k in range(4))
            spots = [shifted(rowed, k - 1, 1) for k in range(4)]
            for col_band in range(2):
                band = 2 * row_band + col_band
                value = sum((0.5 * FILTERS[col_band][k]) * spots[k] for k in range(4))
                value += wavelet_ref[c, band].astype(FULL)
                bands_ref[c, band] = value
                power_ref[band] += value * value

    each(0, channels, analyse)
    powers_ref[chan] = power_ref[...].astype(LOW)
    each(1, chans, lambda d: chan_copy(powers_ref, power_send, power_recv, d).start())

    def sample(c):
        tables = sample_tables(rows_ref[c], base_ref[...])
        spec = recv_spec[:, c].reshape(height, lanes)
        by_cos = contract(spec, tables[:height], 0, 0)
        by_sin = contract(spec, tables[height:], 0, 0)
        real = by_cos[:width] + by_sin[width:]
        imag = by_cos[width:] - by_sin[:width]
        data_ref[c, 0] = (data_ref[c, 0] + 0.5 * (real - obs_ref[c, 0])) / 1.5
        data_ref[c, 1] = (data_ref[c, 1] + 0.5 * (imag - obs_ref[c, 1])) / 1.5

    def finish(chunk):
        each(1, parts, lambda d: piece_copy(1, chunk, d).wait_recv())
        by_group(chunk, sample)

    loads[8].wait()
    for chunk in range(0, min(2, chunks // 2 + 1)):
        finish(chunk)

    def stacked_rows(r):
        if channels % 16 == 0:
            return jnp.concatenate([stack_ref[n, r] for n in range(chans)], 0)
        return jnp.concatenate([stack_ref[n, r].astype(FULL) for n in range(chans)], 0).astype(LOW)

    each(1, chans, lambda d: chan_copy(stack_ref, stack_send, stack_recv, d).wait_recv())
    total = chans * channels
    gram_ref[half] = jnp.zeros((total, total), FULL)

    def gather(g):
        part = 0.0
        for i in range(4):
            rows = stacked_rows(g * 4 + i)
            part = part + contract(rows, rows, 1, 1)
        gram_ref[half] += part

    each(0, own // 4, gather)
    each(1, halves, lambda d: gram_copy(d).start())

    each(1, chans, lambda d: chan_copy(powers_ref, power_send, power_recv, d).wait_recv())
    limit = 0.6 * math.sqrt(CH)
    for band in range(4):
        power = sum(powers_ref[n, band].astype(FULL) for n in range(chans))
        scale_ref[band] = 1.0 / jnp.maximum(1.0, jnp.sqrt(power) / limit)

    def shrink(c):
        wavelet_ref[c] = (bands_ref[c] * scale_ref[...]).astype(LOW)

    each(0, channels, shrink)
    for chunk in range(2, chunks // 2 + 1):
        finish(chunk)

    each(1, halves, lambda d: gram_copy(d).wait_recv())
    gram = sum(gram_ref[h] for h in range(halves))
    diagonal = lax.broadcasted_iota(jnp.int32, (total, total), 0) == lax.broadcasted_iota(
        jnp.int32, (total, total), 1
    )
    trace_sum = jnp.sum(jnp.where(diagonal, gram, 0.0), keepdims=True)
    eye = jnp.where(diagonal, 1.0, 0.0)
    approx = (2.0 / trace_sum) * gram
    root = eye

    def exact(left_side, right_side):
        return jnp.dot(left_side, right_side, precision=HIGH, preferred_element_type=FULL)

    for turn in range(NS_STEPS):
        newton = 1.5 * eye - 0.5 * exact(root, approx)
        approx = exact(approx, newton)
        root = exact(newton, root)
    factor = jnp.sqrt(2.0 * (own * columns * halves) / trace_sum)
    root_ref[...] = root
    mine = root_ref[pl.ds(pl.multiple_of(chan * channels, channels), channels), :].astype(LOW)
    for r in range(own):
        mixed = jnp.dot(mine, stacked_rows(r), preferred_element_type=FULL)
        mixed = factor * mixed
        for j in range(tiles):
            lane_ref[j, pl.ds(r, channels, stride=own), :] = mixed[:, j * 128 : (j + 1) * 128]

    def place_mixed(c):
        start = pl.multiple_of(c * own, own)
        for j in range(tiles):
            mixed_ref[c, :, j * 128 : (j + 1) * 128] = lane_ref[j, pl.ds(start, own), :]

    each(0, channels, place_mixed)

    for chunk in range(chunks // 2 + 1, chunks):
        finish(chunk)

    for chunk in range(chunks):
        for phase in range(2):
            each(1, parts, lambda d: piece_copy(phase, chunk, d).wait_send())
    neighbours(*edges, left)
    neighbours(*rims, left)
    each(1, chans, lambda d: chan_copy(stack_ref, stack_send, stack_recv, d).wait_send())
    each(1, chans, lambda d: chan_copy(powers_ref, power_send, power_recv, d).wait_send())
    each(1, halves, lambda d: gram_copy(d).wait_send())


def write_kernel(*refs):
    count = (len(refs) - 1) // 2
    copies = [
        pltpu.make_async_copy(refs[i], refs[count + i], refs[-1].at[i]) for i in range(count)
    ]
    for copy in copies:
        copy.start()
    for copy in copies:
        copy.wait()


def shards(image, dual_nuclear, dual_wavelet, dual_data, observed, sample_rows):
    channels, own, columns = image.shape
    facets = lax.axis_size("facet")
    halves = lax.axis_size("sub")
    chans = lax.axis_size("chan")
    parts = facets * halves
    height = own * parts
    lanes = 2 * dual_data.shape[2]
    sizes = chunk_sizes(channels)
    chunks = len(sizes)
    total = channels * chans
    bands = dual_wavelet.shape[1]
    here = pl.BlockSpec(memory_space=pltpu.VMEM)
    away = pl.BlockSpec(memory_space=pltpu.HBM)
    rows = sample_rows.reshape(channels, 1, -1)
    base = row_base(height)
    cols = col_base(columns, parts)
    piece = pltpu.VMEM((parts, channels, own, lanes), LOW)
    plane = pltpu.VMEM((channels, columns), LOW)
    planes = pltpu.VMEM((2, channels, columns), LOW)
    wide = pltpu.VMEM((2, channels, columns), FULL)
    dma = pltpu.SemaphoreType.DMA
    outs = (
        (image.shape, FULL), (image.shape, FULL), (dual_wavelet.shape, LOW), (dual_data.shape, FULL),
    )
    operands = [
        pltpu.with_memory_space_constraint(x, pltpu.HBM)
        for x in (rows, image, dual_nuclear, dual_wavelet, dual_data, observed, base, cols)
    ]
    results = pl.pallas_call(
        functools.partial(step_kernel, facets, halves, chans, sizes),
        name="step",
        out_shape=tuple(pltpu.VMEM(*out) for out in outs),
        in_specs=[away] * 8,
        out_specs=[here] * 4,
        scratch_shapes=[
            pltpu.VMEM(rows.shape, jnp.int32), pltpu.VMEM(observed.shape, FULL),
            pltpu.VMEM(base.shape, LOW), pltpu.VMEM(cols.shape, LOW), dma((9,)),
            piece, piece, piece, piece,
            pltpu.VMEM(image.shape, FULL),
            pltpu.VMEM(image.shape, FULL),
            pltpu.VMEM((channels * own, columns), FULL),
            pltpu.VMEM((columns // 128, channels * own, 128), FULL),
            pltpu.VMEM(dual_wavelet.shape, FULL),
            pltpu.VMEM((chans, own, channels, columns), LOW),
            pltpu.VMEM((bands, own, columns), FULL),
            pltpu.VMEM((chans, bands, own, columns), LOW),
            pltpu.VMEM((bands, own, columns), FULL),
            pltpu.VMEM((halves, total, total), FULL),
            pltpu.VMEM((total, total), FULL),
            wide, wide,
            plane, plane, planes, planes, planes, planes, plane, plane,
            dma((2, chunks, parts - 1)), dma((2, chunks, parts - 1)),
            dma((4,)), dma((4,)),
            dma((chans - 1,)), dma((chans - 1,)),
            dma((chans - 1,)), dma((chans - 1,)),
            dma((halves - 1,)), dma((halves - 1,)),
        ],
        compiler_params=pltpu.CompilerParams(
            collective_id=0, has_side_effects=True, vmem_limit_bytes=40000000
        ),
    )(*operands)
    return pl.pallas_call(
        write_kernel,
        name="write",
        out_shape=tuple(jax.ShapeDtypeStruct(*out) for out in outs),
        in_specs=[here] * 4,
        out_specs=[away] * 4,
        scratch_shapes=[dma((4,))],
        compiler_params=pltpu.CompilerParams(vmem_limit_bytes=1000000),
    )(*(pltpu.with_memory_space_constraint(x, pltpu.VMEM) for x in results))


def solution(mesh):
    placed = (
        P(("cube", "chan"), ("facet", "sub"), None),
        P(("cube", "chan"), ("facet", "sub"), None),
        P(("cube", "chan"), None, ("facet", "sub"), None),
        P(("cube", "chan"), None, ("facet", "sub"), None),
        P(("cube", "chan"), None, ("facet", "sub"), None),
        P(("cube", "chan"), None),
    )
    return jax.shard_map(
        shards,
        mesh=mesh,
        in_specs=placed,
        out_specs=(
            P(("cube", "chan"), ("facet", "sub"), None),
            P(("cube", "chan"), ("facet", "sub"), None),
            P(("cube", "chan"), None, ("facet", "sub"), None),
            P(("cube", "chan"), None, ("facet", "sub"), None),
        ),
        check_vma=False,
    )
```

```python
import functools
import math

import jax
import jax.numpy as jnp
import numpy as np
from jax import lax
from jax.experimental import pallas as pl
from jax.experimental.pallas import tpu as pltpu
from jax.sharding import PartitionSpec as P

CH = 64
NS_STEPS = 6


LOWPASS = [0.48296291314453416, 0.8365163037378079, 0.2241438680420134, -0.12940952255126037]
FILTERS = [
    [value / math.sqrt(2.0) for value in LOWPASS],
    [(-1.0) ** index * LOWPASS[3 - index] / math.sqrt(2.0) for index in range(4)],
]
HIGH = lax.Precision.HIGHEST
LOW = jnp.bfloat16
MESH = pl.DeviceIdType.MESH
FULL = jnp.float32


def phase_base(period):
    places = np.arange(period)
    angles = np.float32(2.0 * math.pi / period) * (np.outer(places, places) % period).astype(np.float32)
    norm = np.float32(1.0 / math.sqrt(period))
    return np.cos(angles) * norm, np.sin(angles) * norm


def row_base(height):
    return jnp.asarray(np.concatenate(phase_base(height), 0).astype(LOW))


def col_base(columns, parts):
    cosine, sine = (t.reshape(parts, columns // parts, columns) for t in phase_base(columns))
    return jnp.asarray(np.concatenate([cosine, -sine], 1).astype(LOW))


def sample_tables(rows, base):
    height, samples = base.shape[1], rows.shape[1]
    hot = lax.broadcasted_iota(jnp.int32, (height, samples), 0) == rows
    hot = jnp.where(hot, 1.0, 0.0).astype(LOW)
    both = jnp.dot(base, hot, preferred_element_type=jnp.float32).astype(LOW)
    return jnp.concatenate([both[:height], both[height:]], 1)


def contract(left, right, left_dim, right_dim):
    return lax.dot_general(
        left, right, (((left_dim,), (right_dim,)), ((), ())), preferred_element_type=jnp.float32
    )


def data_step(spec, tables, dual, seen):
    width, samples = dual[0].shape
    both = contract(spec, tables, 0, 0)
    real = both[:width, :samples] + both[width:, samples:]
    imag = both[width:, :samples] - both[:width, samples:]
    return [(d + 0.5 * (v - o)) / 1.5 for d, v, o in zip(dual, (real, imag), seen)]


def shifted(values, offset, axis):
    length = values.shape[axis]
    if offset == 0:
        return values
    place = lax.broadcasted_iota(jnp.int32, values.shape, axis) + offset
    moved = pltpu.roll(values, (-offset) % length, axis)
    return jnp.where((place >= 0) & (place < length), moved, 0.0)


def chunk_sizes(channels):
    if channels % 16 == 0:
        share = channels // 16
        return [2 * share, 5 * share, 5 * share, 4 * share]
    unit = math.gcd(channels, 4)
    return [unit] * (channels // unit)


def step_kernel(
    facets, halves, chans, sizes,
    rows_hbm, image_hbm, nuclear_hbm, wave_hbm, dual_hbm, obs_hbm, base_hbm, cols_hbm,
    next_ref, mixed_ref, wavelet_ref, data_ref, last_spec, last_table, last_obs,
    rows_ref, obs_ref, base_ref, cols_ref, table_ref, load_sem,
    send_back, recv_back, send_spec, recv_spec, synth, field_ref, flat_ref, lane_ref, bands_ref,
    stack_ref, power_ref, powers_ref, scale_ref, gram_ref, root_ref, up_ref, down_ref,
    edge_up, edge_up_in, edge_down, edge_down_in, rim_up, rim_up_in, rim_down, rim_down_in,
    piece_send, piece_recv, edge_send, edge_recv, stack_send, stack_recv,
    power_send, power_recv, gram_send, gram_recv,
):
    parts = facets * halves
    channels, own, columns = next_ref.shape
    height = base_ref.shape[1]
    lanes = send_back.shape[3]
    tiles = columns // 128
    chunks = len(sizes)
    firsts = [sum(sizes[:i]) for i in range(chunks)]
    half = lax.axis_index("sub")
    me = lax.axis_index("facet") * halves + half
    chan = lax.axis_index("chan")

    def place(peer):
        return {"facet": lax.div(peer, halves), "sub": lax.rem(peer, halves)}

    def partner(d):
        if parts & (parts - 1):
            return lax.rem(me + d, parts)
        weights = [1 << bit for bit in range(parts.bit_length() - 1)]
        return sum(
            lax.rem(lax.div(me, weight) + lax.div(d, weight), 2) * weight for weight in weights
        )

    def remote(source, target, sent, received, device):
        return pltpu.make_async_remote_copy(
            src_ref=source, dst_ref=target, send_sem=sent, recv_sem=received,
            device_id=device, device_id_type=MESH,
        )

    def piece_copy(phase, chunk, d):
        source, target = ((send_back, recv_back), (send_spec, recv_spec))[phase]
        peer = partner(d)
        span = pl.ds(firsts[chunk], sizes[chunk])
        return remote(
            source.at[peer, span], target.at[me, span],
            piece_send.at[phase, chunk, d - 1], piece_recv.at[phase, chunk, d - 1], place(peer),
        )

    def chan_copy(buffer, sent, received, d):
        return remote(
            buffer.at[chan], buffer.at[chan], sent.at[d - 1], received.at[d - 1],
            {"chan": lax.rem(chan + d, chans)},
        )

    def gram_copy(d):
        return remote(
            gram_ref.at[half], gram_ref.at[half], gram_send.at[d - 1], gram_recv.at[d - 1],
            {"sub": lax.rem(half + d, halves)},
        )

    def each(low, high, action):
        def run(i, carry):
            action(i)
            return carry

        lax.fori_loop(low, high, run, 0)

    def rim_copy(slot, source, target, up):
        peer = lax.rem(me + (parts - 1 if up else 1), parts)
        return remote(source, target, edge_send.at[slot], edge_recv.at[slot], place(peer))

    def neighbours(slot, up_source, up_target, down_source, down_target, action):
        @pl.when(me > 0)
        def _():
            action(rim_copy(slot, up_source, up_target, True), True)

        @pl.when(me < parts - 1)
        def _():
            action(rim_copy(slot + 1, down_source, down_target, False), False)

    def started(copy, up):
        copy.start()

    def arrived(slot, up_source, up_target, down_source, down_target):
        @pl.when(me < parts - 1)
        def _():
            rim_copy(slot, up_source, up_target, True).wait_recv()

        @pl.when(me > 0)
        def _():
            rim_copy(slot + 1, down_source, down_target, False).wait_recv()

    def left(copy, up):
        copy.wait_send()

    early, late = pl.ds(0, sizes[0]), pl.ds(sizes[0], channels - sizes[0])
    loads = [
        pltpu.make_async_copy(source, target, load_sem.at[i])
        for i, (source, target) in enumerate(
            (
                (rows_hbm, rows_ref), (base_hbm, base_ref),
                (dual_hbm.at[early], data_ref.at[early]), (dual_hbm.at[late], data_ref.at[late]),
                (wave_hbm, wavelet_ref), (cols_hbm, cols_ref), (image_hbm, next_ref),
                (nuclear_hbm, mixed_ref), (obs_hbm, obs_ref),
            )
        )
    ]
    for load in loads[:3]:
        load.start()

    for buffer in (edge_up_in, edge_down_in, rim_up_in, rim_down_in):
        buffer[...] = jnp.zeros_like(buffer)

    barrier = pltpu.get_barrier_semaphore()
    each(
        1, parts,
        lambda d: pl.semaphore_signal(
            barrier, inc=1, device_id=place(lax.rem(me + d, parts)), device_id_type=MESH
        ),
    )
    each(
        1, chans,
        lambda d: pl.semaphore_signal(
            barrier, inc=1, device_id={"chan": lax.rem(chan + d, chans)}, device_id_type=MESH
        ),
    )
    for load in loads[3:]:
        load.start()

    def spread(c):
        tables = sample_tables(rows_ref[c], base_ref[...])
        table_ref[c] = tables
        real = data_ref[c, 0].astype(LOW)
        imag = data_ref[c, 1].astype(LOW)
        pair = jnp.concatenate(
            [jnp.concatenate([real, -imag], 1), jnp.concatenate([imag, real], 1)], 0
        )
        total = contract(tables, pair, 1, 1)
        send_back[:, c] = total.astype(LOW).reshape(parts, own, lanes)

    def by_group(chunk, action):
        pair = math.gcd(sizes[chunk], 4)

        def run(g):
            for i in range(pair):
                action(firsts[chunk] + g * pair + i)

        each(0, sizes[chunk] // pair, run)

    def send_pieces(phase, chunk):
        each(1, parts, lambda d: piece_copy(phase, chunk, d if phase else parts - d).start())

    def wave(c):
        colled = []
        for row_band in range(2):
            first = wavelet_ref[c, 2 * row_band].astype(FULL)
            second = wavelet_ref[c, 2 * row_band + 1].astype(FULL)
            colled.append(
                sum(
                    shifted(FILTERS[0][k] * first + FILTERS[1][k] * second, 1 - k, 1)
                    for k in range(4)
                )
            )
        tapped = [FILTERS[0][k] * colled[0] + FILTERS[1][k] * colled[1] for k in range(4)]
        synth[c] = sum(shifted(tapped[k], 1 - k, 0) for k in range(4))
        up_ref[0, pl.ds(c, 1), :] = tapped[0][0:1]
        below = tapped[2] + pltpu.roll(tapped[3], 1, 0)
        down_ref[0, pl.ds(c, 1), :] = below[own - 1 : own]
        down_ref[1, pl.ds(c, 1), :] = tapped[3][own - 1 : own]

    edges = (0, edge_up, edge_up_in, edge_down, edge_down_in)
    for load in loads[:3]:
        load.wait()
    for chunk in range(chunks):
        if chunk == 1:
            loads[3].wait()
        by_group(chunk, spread)
        if chunk == 0:
            pl.semaphore_wait(barrier, parts + chans - 2)
        send_pieces(0, chunk)
        if chunk == min(1, chunks - 1):
            loads[4].wait()
            each(0, channels, wave)
            edge_up[...] = up_ref[0].astype(LOW)
            edge_down[...] = down_ref[...].astype(LOW)
            neighbours(*edges, started)
    each(0, channels, lambda c: recv_back.__setitem__((me, c), send_back[me, c]))

    for load in loads[5:8]:
        load.wait()
    arrived(*edges)
    up_ref[0] = edge_up_in[...].astype(FULL)
    down_ref[...] = edge_down_in[...].astype(FULL)
    row = lax.broadcasted_iota(jnp.int32, (own, columns), 0)
    group = 2 if lanes == 128 and parts % 2 == 0 else 1

    for chunk in range(chunks):
        each(1, parts, lambda d: piece_copy(0, chunk, d).wait_recv())
        first, block = firsts[chunk], sizes[chunk]
        span = pl.ds(first, block)
        back = 0.0
        for p in range(0, parts, group):
            pieces = [recv_back[p + i, span].reshape(block * own, lanes) for i in range(group)]
            base = cols_ref[p : p + group].reshape(group * lanes, columns)
            back = back + contract(jnp.concatenate(pieces, 1), base, 1, 0)
        flat_ref[pl.ds(first * own, block * own), :] = back

        def update(c):
            start = pl.multiple_of(c * own, own)
            total = flat_ref[pl.ds(start, own), :] + synth[c]
            total += jnp.where(row == own - 1, up_ref[0, pl.ds(c, 1), :], 0.0)
            total += jnp.where(row == 0, down_ref[0, pl.ds(c, 1), :], 0.0)
            total += jnp.where(row == 1, down_ref[1, pl.ds(c, 1), :], 0.0)
            image = next_ref[c]
            nuclear = mixed_ref[c]
            image_next = jnp.maximum(image - 0.5 * (total + nuclear), 0.0)
            field = 2.0 * image_next - image
            next_ref[c] = image_next
            field_ref[c] = field
            stacked = nuclear + field
            for j in range(tiles):
                lane_ref[j, pl.ds(start, own), :] = stacked[:, j * 128 : (j + 1) * 128]
            up_ref[0, pl.ds(c, 1), :] = field[0:1]
            up_ref[1, pl.ds(c, 1), :] = field[1:2]
            down_ref[0, pl.ds(c, 1), :] = field[own - 1 : own]

        each(first, first + block, update)
        low = field_ref[span].reshape(block * own, columns).astype(LOW)
        for p in range(0, parts, group):
            base = cols_ref[p : p + group].reshape(group * lanes, columns)
            spec = contract(low, base, 1, 1).astype(LOW)
            for i in range(group):
                send_spec[p + i, span] = spec[:, i * lanes : (i + 1) * lanes].reshape(
                    block, own, lanes
                )
        if chunk == 0:
            send_pieces(1, chunk)

    rims = (2, rim_up, rim_up_in, rim_down, rim_down_in)
    rim_up[...] = up_ref[...].astype(LOW)
    rim_down[...] = down_ref[0].astype(LOW)
    neighbours(*rims, started)
    for chunk in range(1, chunks):
        send_pieces(1, chunk)

    for r in range(own):
        for j in range(tiles):
            picked = lane_ref[j, pl.ds(r, channels, stride=own), :]
            stack_ref[chan, r, :, j * 128 : (j + 1) * 128] = picked.astype(LOW)
    each(1, chans, lambda d: chan_copy(stack_ref, stack_send, stack_recv, d).start())
    each(0, channels, lambda c: recv_spec.__setitem__((me, c), send_spec[me, c]))
    power_ref[...] = jnp.zeros_like(power_ref)
    arrived(*rims)
    up_ref[...] = rim_up_in[...].astype(FULL)
    down_ref[0] = rim_down_in[...].astype(FULL)

    def analyse(c):
        field = field_ref[c]
        above = down_ref[0, pl.ds(c, 1), :]
        below = up_ref[0, pl.ds(c, 1), :]
        beyond = up_ref[1, pl.ds(c, 1), :]
        moved = [
            jnp.where(row == 0, above, pltpu.roll(field, 1, 0)),
            field,
            jnp.where(row == own - 1, below, pltpu.roll(field, own - 1, 0)),
            jnp.where(
                row == own - 1, beyond,
                jnp.where(row == own - 2, below, pltpu.roll(field, own - 2, 0)),
            ),
        ]
        for row_band in range(2):
            rowed = sum(FILTERS[row_band][k] * moved[k] for k in range(4))
            spots = [shifted(rowed, k - 1, 1) for k in range(4)]
            for col_band in range(2):
                band = 2 * row_band + col_band
                value = sum((0.5 * FILTERS[col_band][k]) * spots[k] for k in range(4))
                value += wavelet_ref[c, band].astype(FULL)
                bands_ref[c, band] = value
                power_ref[band] += value * value

    each(0, channels, analyse)
    powers_ref[chan] = power_ref[...].astype(LOW)
    each(1, chans, lambda d: chan_copy(powers_ref, power_send, power_recv, d).start())

    def sample(c):
        spec = recv_spec[:, c].reshape(height, lanes)
        dual, seen = (data_ref[c, 0], data_ref[c, 1]), (obs_ref[c, 0], obs_ref[c, 1])
        data_ref[c, 0], data_ref[c, 1] = data_step(spec, table_ref[c], dual, seen)

    def finish(chunk):
        each(1, parts, lambda d: piece_copy(1, chunk, d).wait_recv())
        by_group(chunk, sample)

    loads[8].wait()
    ends = [firsts[i] + sizes[i] for i in range(chunks)]
    soon = sum(8 * end <= 3 * channels for end in ends)
    later = sum(3 * end <= 2 * channels for end in ends)
    for chunk in range(soon):
        finish(chunk)

    def stacked_rows(r):
        if channels % 16 == 0:
            return jnp.concatenate([stack_ref[n, r] for n in range(chans)], 0)
        return jnp.concatenate([stack_ref[n, r].astype(FULL) for n in range(chans)], 0).astype(LOW)

    each(1, chans, lambda d: chan_copy(stack_ref, stack_send, stack_recv, d).wait_recv())
    total = chans * channels
    gram_ref[half] = jnp.zeros((total, total), FULL)

    def gather(g):
        part = 0.0
        for i in range(4):
            rows = stacked_rows(g * 4 + i)
            part = part + contract(rows, rows, 1, 1)
        gram_ref[half] += part

    each(0, own // 4, gather)
    each(1, halves, lambda d: gram_copy(d).start())

    each(1, chans, lambda d: chan_copy(powers_ref, power_send, power_recv, d).wait_recv())
    limit = 0.6 * math.sqrt(CH)
    for band in range(4):
        power = sum(powers_ref[n, band].astype(FULL) for n in range(chans))
        scale_ref[band] = 1.0 / jnp.maximum(1.0, jnp.sqrt(power) / limit)

    def shrink(c):
        wavelet_ref[c] = (bands_ref[c] * scale_ref[...]).astype(LOW)

    each(0, channels, shrink)
    for chunk in range(soon, later):
        finish(chunk)

    each(1, halves, lambda d: gram_copy(d).wait_recv())
    gram = sum(gram_ref[h] for h in range(halves))
    diagonal = lax.broadcasted_iota(jnp.int32, (total, total), 0) == lax.broadcasted_iota(
        jnp.int32, (total, total), 1
    )
    trace_sum = jnp.sum(jnp.where(diagonal, gram, 0.0), keepdims=True)
    eye = jnp.where(diagonal, 1.0, 0.0)
    approx = (2.0 / trace_sum) * gram
    root = eye

    def exact(left_side, right_side):
        return jnp.dot(left_side, right_side, precision=HIGH, preferred_element_type=FULL)

    for turn in range(NS_STEPS):
        newton = 1.5 * eye - 0.5 * exact(root, approx)
        approx = exact(approx, newton)
        root = exact(newton, root)
    factor = jnp.sqrt(2.0 * (own * columns * halves) / trace_sum)
    root_ref[...] = root
    mine = root_ref[pl.ds(pl.multiple_of(chan * channels, channels), channels), :].astype(LOW)
    for r in range(own):
        mixed = jnp.dot(mine, stacked_rows(r), preferred_element_type=FULL)
        mixed = factor * mixed
        for j in range(tiles):
            lane_ref[j, pl.ds(r, channels, stride=own), :] = mixed[:, j * 128 : (j + 1) * 128]

    def place_mixed(c):
        start = pl.multiple_of(c * own, own)
        for j in range(tiles):
            mixed_ref[c, :, j * 128 : (j + 1) * 128] = lane_ref[j, pl.ds(start, own), :]

    each(0, channels, place_mixed)

    tail = pl.ds(firsts[-1], sizes[-1])
    last_table[...] = table_ref[tail]
    last_obs[...] = obs_ref[tail]
    for chunk in range(later, chunks - 1):
        finish(chunk)
    each(1, parts, lambda d: piece_copy(1, chunks - 1, d).wait_recv())
    last_spec[...] = recv_spec[:, tail]

    for chunk in range(chunks):
        for phase in range(2):
            each(1, parts, lambda d: piece_copy(phase, chunk, d).wait_send())
    neighbours(*edges, left)
    neighbours(*rims, left)
    each(1, chans, lambda d: chan_copy(stack_ref, stack_send, stack_recv, d).wait_send())
    each(1, chans, lambda d: chan_copy(powers_ref, power_send, power_recv, d).wait_send())
    each(1, halves, lambda d: gram_copy(d).wait_send())


def write_kernel(
    next_ref, mixed_ref, wavelet_ref, data_ref, spec_ref, table_ref, obs_ref,
    next_hbm, mixed_hbm, wavelet_hbm, data_hbm, done_ref, sem,
):
    parts, count, own, lanes = spec_ref.shape
    first = data_ref.shape[0] - count
    early, late = pl.ds(0, first), pl.ds(first, count)
    copies = [
        pltpu.make_async_copy(source, target, sem.at[i])
        for i, (source, target) in enumerate(
            (
                (next_ref, next_hbm), (mixed_ref, mixed_hbm), (wavelet_ref, wavelet_hbm),
                (data_ref.at[early], data_hbm.at[early]), (done_ref, data_hbm.at[late]),
            )
        )
    ]
    for copy in copies[:4]:
        copy.start()
    for i in range(count):
        c = first + i
        spec = spec_ref[:, i].reshape(parts * own, lanes)
        dual, seen = (data_ref[c, 0], data_ref[c, 1]), (obs_ref[i, 0], obs_ref[i, 1])
        done_ref[i, 0], done_ref[i, 1] = data_step(spec, table_ref[i], dual, seen)
    copies[4].start()
    for copy in copies:
        copy.wait()


def shards(image, dual_nuclear, dual_wavelet, dual_data, observed, sample_rows):
    channels, own, columns = image.shape
    facets = lax.axis_size("facet")
    halves = lax.axis_size("sub")
    chans = lax.axis_size("chan")
    parts = facets * halves
    height = own * parts
    lanes = 2 * dual_data.shape[2]
    sizes = chunk_sizes(channels)
    chunks = len(sizes)
    total = channels * chans
    bands = dual_wavelet.shape[1]
    here = pl.BlockSpec(memory_space=pltpu.VMEM)
    away = pl.BlockSpec(memory_space=pltpu.HBM)
    rows = sample_rows.reshape(channels, 1, -1)
    base = row_base(height)
    cols = col_base(columns, parts)
    piece = pltpu.VMEM((parts, channels, own, lanes), LOW)
    plane = pltpu.VMEM((channels, columns), LOW)
    planes = pltpu.VMEM((2, channels, columns), LOW)
    wide = pltpu.VMEM((2, channels, columns), FULL)
    dma = pltpu.SemaphoreType.DMA
    last = sizes[-1]
    table = (height, 2 * dual_data.shape[3])
    outs = (
        (image.shape, FULL), (image.shape, FULL), (dual_wavelet.shape, LOW), (dual_data.shape, FULL),
    )
    handed = (
        ((parts, last, own, lanes), LOW), ((last, *table), LOW), ((last, *observed.shape[1:]), FULL),
    )
    operands = [
        pltpu.with_memory_space_constraint(x, pltpu.HBM)
        for x in (rows, image, dual_nuclear, dual_wavelet, dual_data, observed, base, cols)
    ]
    results = pl.pallas_call(
        functools.partial(step_kernel, facets, halves, chans, sizes),
        name="step",
        out_shape=tuple(pltpu.VMEM(*out) for out in outs + handed),
        in_specs=[away] * 8,
        out_specs=[here] * 7,
        scratch_shapes=[
            pltpu.VMEM(rows.shape, jnp.int32), pltpu.VMEM(observed.shape, FULL),
            pltpu.VMEM(base.shape, LOW), pltpu.VMEM(cols.shape, LOW),
            pltpu.VMEM((channels, *table), LOW), dma((9,)),
            piece, piece, piece, piece,
            pltpu.VMEM(image.shape, FULL),
            pltpu.VMEM(image.shape, FULL),
            pltpu.VMEM((channels * own, columns), FULL),
            pltpu.VMEM((columns // 128, channels * own, 128), FULL),
            pltpu.VMEM(dual_wavelet.shape, FULL),
            pltpu.VMEM((chans, own, channels, columns), LOW),
            pltpu.VMEM((bands, own, columns), FULL),
            pltpu.VMEM((chans, bands, own, columns), LOW),
            pltpu.VMEM((bands, own, columns), FULL),
            pltpu.VMEM((halves, total, total), FULL),
            pltpu.VMEM((total, total), FULL),
            wide, wide,
            plane, plane, planes, planes, planes, planes, plane, plane,
            dma((2, chunks, parts - 1)), dma((2, chunks, parts - 1)),
            dma((4,)), dma((4,)),
            dma((chans - 1,)), dma((chans - 1,)),
            dma((chans - 1,)), dma((chans - 1,)),
            dma((halves - 1,)), dma((halves - 1,)),
        ],
        compiler_params=pltpu.CompilerParams(
            collective_id=0, has_side_effects=True, vmem_limit_bytes=44000000
        ),
    )(*operands)
    return pl.pallas_call(
        write_kernel,
        name="write",
        out_shape=tuple(jax.ShapeDtypeStruct(*out) for out in outs),
        in_specs=[here] * 7,
        out_specs=[away] * 4,
        scratch_shapes=[pltpu.VMEM((last, *observed.shape[1:]), FULL), dma((5,))],
        compiler_params=pltpu.CompilerParams(vmem_limit_bytes=3000000),
    )(*(pltpu.with_memory_space_constraint(x, pltpu.VMEM) for x in results))


def solution(mesh):
    placed = (
        P(("cube", "chan"), ("facet", "sub"), None),
        P(("cube", "chan"), ("facet", "sub"), None),
        P(("cube", "chan"), None, ("facet", "sub"), None),
        P(("cube", "chan"), None, ("facet", "sub"), None),
        P(("cube", "chan"), None, ("facet", "sub"), None),
        P(("cube", "chan"), None),
    )
    return jax.shard_map(
        shards,
        mesh=mesh,
        in_specs=placed,
        out_specs=(
            P(("cube", "chan"), ("facet", "sub"), None),
            P(("cube", "chan"), ("facet", "sub"), None),
            P(("cube", "chan"), None, ("facet", "sub"), None),
            P(("cube", "chan"), None, ("facet", "sub"), None),
        ),
        check_vma=False,
    )
```

```python
import functools
import math

import jax
import jax.numpy as jnp
import numpy as np
from jax import lax
from jax.experimental import pallas as pl
from jax.experimental.pallas import tpu as pltpu
from jax.sharding import PartitionSpec as P

CH = 64
NS_STEPS = 6


LOWPASS = [0.48296291314453416, 0.8365163037378079, 0.2241438680420134, -0.12940952255126037]
FILTERS = [
    [value / math.sqrt(2.0) for value in LOWPASS],
    [(-1.0) ** index * LOWPASS[3 - index] / math.sqrt(2.0) for index in range(4)],
]
HIGH = lax.Precision.HIGHEST
LOW = jnp.bfloat16
MESH = pl.DeviceIdType.MESH
FULL = jnp.float32


def phase_base(period):
    places = np.arange(period)
    angles = np.float32(2.0 * math.pi / period) * (np.outer(places, places) % period).astype(np.float32)
    norm = np.float32(1.0 / math.sqrt(period))
    return np.cos(angles) * norm, np.sin(angles) * norm


def row_base(height):
    return jnp.asarray(np.concatenate(phase_base(height), 0).astype(LOW))


def col_base(columns, parts):
    cosine, sine = (t.reshape(parts, columns // parts, columns) for t in phase_base(columns))
    return jnp.asarray(np.concatenate([cosine, -sine], 1).astype(LOW))


def sample_tables(rows, base):
    height, samples = base.shape[1], rows.shape[1]
    hot = lax.broadcasted_iota(jnp.int32, (height, samples), 0) == rows
    hot = jnp.where(hot, 1.0, 0.0).astype(LOW)
    both = jnp.dot(base, hot, preferred_element_type=jnp.float32).astype(LOW)
    return jnp.concatenate([both[:height], both[height:]], 1)


def contract(left, right, left_dim, right_dim):
    return lax.dot_general(
        left, right, (((left_dim,), (right_dim,)), ((), ())), preferred_element_type=jnp.float32
    )


def data_step(spec, tables, dual, seen):
    width, samples = dual[0].shape
    both = contract(spec, tables, 0, 0)
    real = both[:width, :samples] + both[width:, samples:]
    imag = both[width:, :samples] - both[:width, samples:]
    return [(d + 0.5 * (v - o)) / 1.5 for d, v, o in zip(dual, (real, imag), seen)]


def shifted(values, offset, axis):
    length = values.shape[axis]
    if offset == 0:
        return values
    place = lax.broadcasted_iota(jnp.int32, values.shape, axis) + offset
    moved = pltpu.roll(values, (-offset) % length, axis)
    return jnp.where((place >= 0) & (place < length), moved, 0.0)


def chunk_sizes(channels):
    if channels % 16 == 0:
        share = channels // 16
        return ([2 * share, 6 * share, 8 * share],) * 2
    unit = math.gcd(channels, 4)
    return ([unit] * (channels // unit),) * 2


def step_kernel(
    facets, halves, chans, sizes,
    rows_hbm, image_hbm, nuclear_hbm, wave_hbm, dual_hbm, obs_hbm, base_hbm, cols_hbm,
    next_ref, mixed_ref, wavelet_ref, data_ref, last_spec, last_table, last_obs,
    rows_ref, obs_ref, base_ref, cols_ref, table_ref, load_sem,
    send_back, recv_back, send_spec, recv_spec, synth, field_ref, flat_ref, lane_ref, bands_ref,
    stack_ref, power_ref, powers_ref, scale_ref, gram_ref, root_ref, up_ref, down_ref,
    edge_up, edge_up_in, edge_down, edge_down_in, rim_up, rim_up_in, rim_down, rim_down_in,
    piece_send, piece_recv, edge_send, edge_recv, stack_send, stack_recv,
    power_send, power_recv, gram_send, gram_recv,
):
    parts = facets * halves
    channels, own, columns = next_ref.shape
    height = base_ref.shape[1]
    lanes = send_back.shape[3]
    tiles = columns // 128
    counts = [len(of_phase) for of_phase in sizes]
    firsts = [[sum(of_phase[:i]) for i in range(len(of_phase))] for of_phase in sizes]
    half = lax.axis_index("sub")
    me = lax.axis_index("facet") * halves + half
    chan = lax.axis_index("chan")

    def place(peer):
        return {"facet": lax.div(peer, halves), "sub": lax.rem(peer, halves)}

    def remote(source, target, sent, received, device):
        return pltpu.make_async_remote_copy(
            src_ref=source, dst_ref=target, send_sem=sent, recv_sem=received,
            device_id=device, device_id_type=MESH,
        )

    def piece_copy(phase, chunk, d):
        source, target = ((send_back, recv_back), (send_spec, recv_spec))[phase]
        peer = lax.rem(me + d, parts)
        span = pl.ds(firsts[phase][chunk], sizes[phase][chunk])
        return remote(
            source.at[peer, span], target.at[me, span],
            piece_send.at[phase, chunk, d - 1], piece_recv.at[phase, chunk, d - 1], place(peer),
        )

    def chan_copy(buffer, sent, received, d):
        return remote(
            buffer.at[chan], buffer.at[chan], sent.at[d - 1], received.at[d - 1],
            {"chan": lax.rem(chan + d, chans)},
        )

    def gram_copy(d):
        return remote(
            gram_ref.at[half], gram_ref.at[half], gram_send.at[d - 1], gram_recv.at[d - 1],
            {"sub": lax.rem(half + d, halves)},
        )

    def each(low, high, action):
        def run(i, carry):
            action(i)
            return carry

        lax.fori_loop(low, high, run, 0)

    def rim_copy(slot, source, target, up):
        peer = lax.rem(me + (parts - 1 if up else 1), parts)
        return remote(source, target, edge_send.at[slot], edge_recv.at[slot], place(peer))

    def neighbours(slot, up_source, up_target, down_source, down_target, action):
        @pl.when(me > 0)
        def _():
            action(rim_copy(slot, up_source, up_target, True), True)

        @pl.when(me < parts - 1)
        def _():
            action(rim_copy(slot + 1, down_source, down_target, False), False)

    def started(copy, up):
        copy.start()

    def arrived(slot, up_source, up_target, down_source, down_target):
        @pl.when(me < parts - 1)
        def _():
            rim_copy(slot, up_source, up_target, True).wait_recv()

        @pl.when(me > 0)
        def _():
            rim_copy(slot + 1, down_source, down_target, False).wait_recv()

    def left(copy, up):
        copy.wait_send()

    early, late = pl.ds(0, sizes[0][0]), pl.ds(sizes[0][0], channels - sizes[0][0])
    loads = [
        pltpu.make_async_copy(source, target, load_sem.at[i])
        for i, (source, target) in enumerate(
            (
                (rows_hbm, rows_ref), (base_hbm, base_ref),
                (dual_hbm.at[early], data_ref.at[early]), (dual_hbm.at[late], data_ref.at[late]),
                (wave_hbm, wavelet_ref), (cols_hbm, cols_ref), (image_hbm, next_ref),
                (nuclear_hbm, mixed_ref), (obs_hbm, obs_ref),
            )
        )
    ]
    for load in loads[:3]:
        load.start()

    for buffer in (edge_up_in, edge_down_in, rim_up_in, rim_down_in):
        buffer[...] = jnp.zeros_like(buffer)

    barrier = pltpu.get_barrier_semaphore()
    each(
        1, parts,
        lambda d: pl.semaphore_signal(
            barrier, inc=1, device_id=place(lax.rem(me + d, parts)), device_id_type=MESH
        ),
    )
    each(
        1, chans,
        lambda d: pl.semaphore_signal(
            barrier, inc=1, device_id={"chan": lax.rem(chan + d, chans)}, device_id_type=MESH
        ),
    )
    loads[3].start()

    def spread(c):
        tables = sample_tables(rows_ref[c], base_ref[...])
        table_ref[c] = tables
        real = data_ref[c, 0].astype(LOW)
        imag = data_ref[c, 1].astype(LOW)
        pair = jnp.concatenate(
            [jnp.concatenate([real, -imag], 1), jnp.concatenate([imag, real], 1)], 0
        )
        total = contract(tables, pair, 1, 1)
        send_back[:, c] = total.astype(LOW).reshape(parts, own, lanes)

    def by_group(phase, chunk, action):
        first, count = firsts[phase][chunk], sizes[phase][chunk]
        pair = math.gcd(count, 4)

        def run(g):
            for i in range(pair):
                action(first + g * pair + i)

        each(0, count // pair, run)

    def send_pieces(phase, chunk):
        each(1, parts, lambda d: piece_copy(phase, chunk, d).start())

    def wave(c):
        colled = []
        for row_band in range(2):
            first = wavelet_ref[c, 2 * row_band].astype(FULL)
            second = wavelet_ref[c, 2 * row_band + 1].astype(FULL)
            colled.append(
                sum(
                    shifted(FILTERS[0][k] * first + FILTERS[1][k] * second, 1 - k, 1)
                    for k in range(4)
                )
            )
        tapped = [FILTERS[0][k] * colled[0] + FILTERS[1][k] * colled[1] for k in range(4)]
        synth[c] = sum(shifted(tapped[k], 1 - k, 0) for k in range(4))
        up_ref[0, pl.ds(c, 1), :] = tapped[0][0:1]
        below = tapped[2] + pltpu.roll(tapped[3], 1, 0)
        down_ref[0, pl.ds(c, 1), :] = below[own - 1 : own]
        down_ref[1, pl.ds(c, 1), :] = tapped[3][own - 1 : own]

    edges = (0, edge_up, edge_up_in, edge_down, edge_down_in)
    for load in loads[:3]:
        load.wait()
    for chunk in range(counts[0]):
        if chunk == 1:
            loads[3].wait()
        by_group(0, chunk, spread)
        if chunk == 0:
            pl.semaphore_wait(barrier, parts + chans - 2)
        send_pieces(0, chunk)
        if chunk == 0:
            for load in loads[4:]:
                load.start()
        if chunk == min(1, counts[0] - 1):
            loads[4].wait()
            each(0, channels, wave)
            edge_up[...] = up_ref[0].astype(LOW)
            edge_down[...] = down_ref[...].astype(LOW)
            neighbours(*edges, started)
    each(0, channels, lambda c: recv_back.__setitem__((me, c), send_back[me, c]))

    for load in loads[5:8]:
        load.wait()
    arrived(*edges)
    up_ref[0] = edge_up_in[...].astype(FULL)
    down_ref[...] = edge_down_in[...].astype(FULL)
    row = lax.broadcasted_iota(jnp.int32, (own, columns), 0)
    group = 2 if lanes == 128 and parts % 2 == 0 else 1

    for chunk in range(counts[0]):
        each(1, parts, lambda d: piece_copy(0, chunk, d).wait_recv())
        first, block = firsts[0][chunk], sizes[0][chunk]
        span = pl.ds(first, block)
        back = 0.0
        for p in range(0, parts, group):
            pieces = [recv_back[p + i, span].reshape(block * own, lanes) for i in range(group)]
            base = cols_ref[p : p + group].reshape(group * lanes, columns)
            back = back + contract(jnp.concatenate(pieces, 1), base, 1, 0)
        flat_ref[pl.ds(first * own, block * own), :] = back

        def update(c):
            start = pl.multiple_of(c * own, own)
            total = flat_ref[pl.ds(start, own), :] + synth[c]
            total += jnp.where(row == own - 1, up_ref[0, pl.ds(c, 1), :], 0.0)
            total += jnp.where(row == 0, down_ref[0, pl.ds(c, 1), :], 0.0)
            total += jnp.where(row == 1, down_ref[1, pl.ds(c, 1), :], 0.0)
            image = next_ref[c]
            nuclear = mixed_ref[c]
            image_next = jnp.maximum(image - 0.5 * (total + nuclear), 0.0)
            field = 2.0 * image_next - image
            next_ref[c] = image_next
            field_ref[c] = field
            stacked = nuclear + field
            for j in range(tiles):
                lane_ref[j, pl.ds(start, own), :] = stacked[:, j * 128 : (j + 1) * 128]
            up_ref[0, pl.ds(c, 1), :] = field[0:1]
            up_ref[1, pl.ds(c, 1), :] = field[1:2]
            down_ref[0, pl.ds(c, 1), :] = field[own - 1 : own]

        each(first, first + block, update)
        low = field_ref[span].reshape(block * own, columns).astype(LOW)
        for p in range(0, parts, group):
            base = cols_ref[p : p + group].reshape(group * lanes, columns)
            spec = contract(low, base, 1, 1).astype(LOW)
            for i in range(group):
                send_spec[p + i, span] = spec[:, i * lanes : (i + 1) * lanes].reshape(
                    block, own, lanes
                )
        if chunk == 0:
            send_pieces(1, chunk)

    rims = (2, rim_up, rim_up_in, rim_down, rim_down_in)
    rim_up[...] = up_ref[...].astype(LOW)
    rim_down[...] = down_ref[0].astype(LOW)
    neighbours(*rims, started)
    for chunk in range(1, counts[1]):
        send_pieces(1, chunk)

    for r in range(own):
        for j in range(tiles):
            picked = lane_ref[j, pl.ds(r, channels, stride=own), :]
            stack_ref[chan, r, :, j * 128 : (j + 1) * 128] = picked.astype(LOW)
    each(1, chans, lambda d: chan_copy(stack_ref, stack_send, stack_recv, d).start())
    each(0, channels, lambda c: recv_spec.__setitem__((me, c), send_spec[me, c]))
    power_ref[...] = jnp.zeros_like(power_ref)
    arrived(*rims)
    up_ref[...] = rim_up_in[...].astype(FULL)
    down_ref[0] = rim_down_in[...].astype(FULL)

    def analyse(c):
        field = field_ref[c]
        above = down_ref[0, pl.ds(c, 1), :]
        below = up_ref[0, pl.ds(c, 1), :]
        beyond = up_ref[1, pl.ds(c, 1), :]
        moved = [
            jnp.where(row == 0, above, pltpu.roll(field, 1, 0)),
            field,
            jnp.where(row == own - 1, below, pltpu.roll(field, own - 1, 0)),
            jnp.where(
                row == own - 1, beyond,
                jnp.where(row == own - 2, below, pltpu.roll(field, own - 2, 0)),
            ),
        ]
        for row_band in range(2):
            rowed = sum(FILTERS[row_band][k] * moved[k] for k in range(4))
            spots = [shifted(rowed, k - 1, 1) for k in range(4)]
            for col_band in range(2):
                band = 2 * row_band + col_band
                value = sum((0.5 * FILTERS[col_band][k]) * spots[k] for k in range(4))
                value += wavelet_ref[c, band].astype(FULL)
                bands_ref[c, band] = value
                power_ref[band] += value * value

    each(0, channels, analyse)
    powers_ref[chan] = power_ref[...].astype(LOW)
    each(1, chans, lambda d: chan_copy(powers_ref, power_send, power_recv, d).start())

    def sample(c):
        spec = recv_spec[:, c].reshape(height, lanes)
        dual, seen = (data_ref[c, 0], data_ref[c, 1]), (obs_ref[c, 0], obs_ref[c, 1])
        data_ref[c, 0], data_ref[c, 1] = data_step(spec, table_ref[c], dual, seen)

    def finish(chunk):
        each(1, parts, lambda d: piece_copy(1, chunk, d).wait_recv())
        by_group(1, chunk, sample)

    loads[8].wait()
    ends = [first + count for first, count in zip(firsts[1], sizes[1])]
    soon = sum(8 * end <= 3 * channels for end in ends)
    later = sum(3 * end <= 2 * channels for end in ends)
    for chunk in range(soon):
        finish(chunk)

    def stacked_rows(r):
        if channels % 16 == 0:
            return jnp.concatenate([stack_ref[n, r] for n in range(chans)], 0)
        return jnp.concatenate([stack_ref[n, r].astype(FULL) for n in range(chans)], 0).astype(LOW)

    each(1, chans, lambda d: chan_copy(stack_ref, stack_send, stack_recv, d).wait_recv())
    total = chans * channels
    gram_ref[half] = jnp.zeros((total, total), FULL)

    def gather(g):
        part = 0.0
        for i in range(4):
            rows = stacked_rows(g * 4 + i)
            part = part + contract(rows, rows, 1, 1)
        gram_ref[half] += part

    each(0, own // 4, gather)
    each(1, halves, lambda d: gram_copy(d).start())

    each(1, chans, lambda d: chan_copy(powers_ref, power_send, power_recv, d).wait_recv())
    limit = 0.6 * math.sqrt(CH)
    for band in range(4):
        power = sum(powers_ref[n, band].astype(FULL) for n in range(chans))
        scale_ref[band] = 1.0 / jnp.maximum(1.0, jnp.sqrt(power) / limit)

    def shrink(c):
        wavelet_ref[c] = (bands_ref[c] * scale_ref[...]).astype(LOW)

    each(0, channels, shrink)
    for chunk in range(soon, later):
        finish(chunk)

    each(1, halves, lambda d: gram_copy(d).wait_recv())
    gram = sum(gram_ref[h] for h in range(halves))
    diagonal = lax.broadcasted_iota(jnp.int32, (total, total), 0) == lax.broadcasted_iota(
        jnp.int32, (total, total), 1
    )
    trace_sum = jnp.sum(jnp.where(diagonal, gram, 0.0), keepdims=True)
    eye = jnp.where(diagonal, 1.0, 0.0)
    approx = (2.0 / trace_sum) * gram
    root = eye

    def exact(left_side, right_side):
        return jnp.dot(left_side, right_side, precision=HIGH, preferred_element_type=FULL)

    for turn in range(NS_STEPS):
        newton = 1.5 * eye - 0.5 * exact(root, approx)
        approx = exact(approx, newton)
        root = exact(newton, root)
    factor = jnp.sqrt(2.0 * (own * columns * halves) / trace_sum)
    root_ref[...] = root
    mine = root_ref[pl.ds(pl.multiple_of(chan * channels, channels), channels), :].astype(LOW)
    for r in range(own):
        mixed = jnp.dot(mine, stacked_rows(r), preferred_element_type=FULL)
        mixed = factor * mixed
        for j in range(tiles):
            lane_ref[j, pl.ds(r, channels, stride=own), :] = mixed[:, j * 128 : (j + 1) * 128]

    def place_mixed(c):
        start = pl.multiple_of(c * own, own)
        for j in range(tiles):
            mixed_ref[c, :, j * 128 : (j + 1) * 128] = lane_ref[j, pl.ds(start, own), :]

    each(0, channels, place_mixed)

    tail = pl.ds(firsts[1][-1], sizes[1][-1])
    last_table[...] = table_ref[tail]
    last_obs[...] = obs_ref[tail]
    for chunk in range(later, counts[1] - 1):
        finish(chunk)
    each(1, parts, lambda d: piece_copy(1, counts[1] - 1, d).wait_recv())
    last_spec[...] = recv_spec[:, tail]

    for phase in range(2):
        for chunk in range(counts[phase]):
            each(1, parts, lambda d: piece_copy(phase, chunk, d).wait_send())
    neighbours(*edges, left)
    neighbours(*rims, left)
    each(1, chans, lambda d: chan_copy(stack_ref, stack_send, stack_recv, d).wait_send())
    each(1, chans, lambda d: chan_copy(powers_ref, power_send, power_recv, d).wait_send())
    each(1, halves, lambda d: gram_copy(d).wait_send())


def write_kernel(
    next_ref, mixed_ref, wavelet_ref, data_ref, spec_ref, table_ref, obs_ref,
    next_hbm, mixed_hbm, wavelet_hbm, data_hbm, done_ref, sem,
):
    parts, count, own, lanes = spec_ref.shape
    first = data_ref.shape[0] - count
    early, late = pl.ds(0, first), pl.ds(first, count)
    copies = [
        pltpu.make_async_copy(source, target, sem.at[i])
        for i, (source, target) in enumerate(
            (
                (next_ref, next_hbm), (mixed_ref, mixed_hbm), (wavelet_ref, wavelet_hbm),
                (data_ref.at[early], data_hbm.at[early]), (done_ref, data_hbm.at[late]),
            )
        )
    ]
    for copy in copies[:4]:
        copy.start()
    for i in range(count):
        c = first + i
        spec = spec_ref[:, i].reshape(parts * own, lanes)
        dual, seen = (data_ref[c, 0], data_ref[c, 1]), (obs_ref[i, 0], obs_ref[i, 1])
        done_ref[i, 0], done_ref[i, 1] = data_step(spec, table_ref[i], dual, seen)
    copies[4].start()
    for copy in copies:
        copy.wait()


def shards(image, dual_nuclear, dual_wavelet, dual_data, observed, sample_rows):
    channels, own, columns = image.shape
    facets = lax.axis_size("facet")
    halves = lax.axis_size("sub")
    chans = lax.axis_size("chan")
    parts = facets * halves
    height = own * parts
    lanes = 2 * dual_data.shape[2]
    sizes = chunk_sizes(channels)
    chunks = max(len(of_phase) for of_phase in sizes)
    total = channels * chans
    bands = dual_wavelet.shape[1]
    here = pl.BlockSpec(memory_space=pltpu.VMEM)
    away = pl.BlockSpec(memory_space=pltpu.HBM)
    rows = sample_rows.reshape(channels, 1, -1)
    base = row_base(height)
    cols = col_base(columns, parts)
    piece = pltpu.VMEM((parts, channels, own, lanes), LOW)
    plane = pltpu.VMEM((channels, columns), LOW)
    planes = pltpu.VMEM((2, channels, columns), LOW)
    wide = pltpu.VMEM((2, channels, columns), FULL)
    dma = pltpu.SemaphoreType.DMA
    last = sizes[1][-1]
    table = (height, 2 * dual_data.shape[3])
    outs = (
        (image.shape, FULL), (image.shape, FULL), (dual_wavelet.shape, LOW), (dual_data.shape, FULL),
    )
    handed = (
        ((parts, last, own, lanes), LOW), ((last, *table), LOW), ((last, *observed.shape[1:]), FULL),
    )
    operands = [
        pltpu.with_memory_space_constraint(x, pltpu.HBM)
        for x in (rows, image, dual_nuclear, dual_wavelet, dual_data, observed, base, cols)
    ]
    results = pl.pallas_call(
        functools.partial(step_kernel, facets, halves, chans, sizes),
        name="step",
        out_shape=tuple(pltpu.VMEM(*out) for out in outs + handed),
        in_specs=[away] * 8,
        out_specs=[here] * 7,
        scratch_shapes=[
            pltpu.VMEM(rows.shape, jnp.int32), pltpu.VMEM(observed.shape, FULL),
            pltpu.VMEM(base.shape, LOW), pltpu.VMEM(cols.shape, LOW),
            pltpu.VMEM((channels, *table), LOW), dma((9,)),
            piece, piece, piece, piece,
            pltpu.VMEM(image.shape, FULL),
            pltpu.VMEM(image.shape, FULL),
            pltpu.VMEM((channels * own, columns), FULL),
            pltpu.VMEM((columns // 128, channels * own, 128), FULL),
            pltpu.VMEM(dual_wavelet.shape, FULL),
            pltpu.VMEM((chans, own, channels, columns), LOW),
            pltpu.VMEM((bands, own, columns), FULL),
            pltpu.VMEM((chans, bands, own, columns), LOW),
            pltpu.VMEM((bands, own, columns), FULL),
            pltpu.VMEM((halves, total, total), FULL),
            pltpu.VMEM((total, total), FULL),
            wide, wide,
            plane, plane, planes, planes, planes, planes, plane, plane,
            dma((2, chunks, parts - 1)), dma((2, chunks, parts - 1)),
            dma((4,)), dma((4,)),
            dma((chans - 1,)), dma((chans - 1,)),
            dma((chans - 1,)), dma((chans - 1,)),
            dma((halves - 1,)), dma((halves - 1,)),
        ],
        compiler_params=pltpu.CompilerParams(
            collective_id=0, has_side_effects=True, vmem_limit_bytes=44000000
        ),
    )(*operands)
    return pl.pallas_call(
        write_kernel,
        name="write",
        out_shape=tuple(jax.ShapeDtypeStruct(*out) for out in outs),
        in_specs=[here] * 7,
        out_specs=[away] * 4,
        scratch_shapes=[pltpu.VMEM((last, *observed.shape[1:]), FULL), dma((5,))],
        compiler_params=pltpu.CompilerParams(vmem_limit_bytes=3000000),
    )(*(pltpu.with_memory_space_constraint(x, pltpu.VMEM) for x in results))


def solution(mesh):
    placed = (
        P(("cube", "chan"), ("facet", "sub"), None),
        P(("cube", "chan"), ("facet", "sub"), None),
        P(("cube", "chan"), None, ("facet", "sub"), None),
        P(("cube", "chan"), None, ("facet", "sub"), None),
        P(("cube", "chan"), None, ("facet", "sub"), None),
        P(("cube", "chan"), None),
    )
    return jax.shard_map(
        shards,
        mesh=mesh,
        in_specs=placed,
        out_specs=(
            P(("cube", "chan"), ("facet", "sub"), None),
            P(("cube", "chan"), ("facet", "sub"), None),
            P(("cube", "chan"), None, ("facet", "sub"), None),
            P(("cube", "chan"), None, ("facet", "sub"), None),
        ),
        check_vma=False,
    )
```

```python
import functools
import math

import jax
import jax.numpy as jnp
import numpy as np
from jax import lax
from jax.experimental import pallas as pl
from jax.experimental.pallas import tpu as pltpu
from jax.sharding import PartitionSpec as P

CH = 64
NS_STEPS = 6


LOWPASS = [0.48296291314453416, 0.8365163037378079, 0.2241438680420134, -0.12940952255126037]
FILTERS = [
    [value / math.sqrt(2.0) for value in LOWPASS],
    [(-1.0) ** index * LOWPASS[3 - index] / math.sqrt(2.0) for index in range(4)],
]
HIGH = lax.Precision.HIGHEST
LOW = jnp.bfloat16
MESH = pl.DeviceIdType.MESH
FULL = jnp.float32


def phase_base(period):
    places = np.arange(period)
    angles = np.float32(2.0 * math.pi / period) * (np.outer(places, places) % period).astype(np.float32)
    norm = np.float32(1.0 / math.sqrt(period))
    return np.cos(angles) * norm, np.sin(angles) * norm


def row_base(height):
    return jnp.asarray(np.concatenate(phase_base(height), 0).astype(LOW))


def col_base(columns, parts):
    cosine, sine = (t.reshape(parts, columns // parts, columns) for t in phase_base(columns))
    return jnp.asarray(np.concatenate([cosine, -sine], 1).astype(LOW))


def sample_tables(rows, base):
    height, samples = base.shape[1], rows.shape[1]
    hot = lax.broadcasted_iota(jnp.int32, (height, samples), 0) == rows
    hot = jnp.where(hot, 1.0, 0.0).astype(LOW)
    both = jnp.dot(base, hot, preferred_element_type=jnp.float32).astype(LOW)
    return jnp.concatenate([both[:height], both[height:]], 1)


def contract(left, right, left_dim, right_dim):
    return lax.dot_general(
        left, right, (((left_dim,), (right_dim,)), ((), ())), preferred_element_type=jnp.float32
    )


def data_step(spec, tables, dual, seen):
    width, samples = dual[0].shape
    both = contract(spec, tables, 0, 0)
    real = both[:width, :samples] + both[width:, samples:]
    imag = both[width:, :samples] - both[:width, samples:]
    return [(d + 0.5 * (v - o)) / 1.5 for d, v, o in zip(dual, (real, imag), seen)]


def shifted(values, offset, axis):
    length = values.shape[axis]
    if offset == 0:
        return values
    place = lax.broadcasted_iota(jnp.int32, values.shape, axis) + offset
    moved = pltpu.roll(values, (-offset) % length, axis)
    return jnp.where((place >= 0) & (place < length), moved, 0.0)


def chunk_sizes(channels):
    if channels % 16 == 0:
        share = channels // 16
        return ([2 * share, 7 * share, 7 * share],) * 2
    unit = math.gcd(channels, 4)
    return ([unit] * (channels // unit),) * 2


def step_kernel(
    facets, halves, chans, sizes,
    rows_hbm, image_hbm, nuclear_hbm, wave_hbm, dual_hbm, obs_hbm, base_hbm, cols_hbm,
    next_ref, mixed_ref, wavelet_ref, data_ref, last_spec, last_table, last_obs,
    rows_ref, obs_ref, base_ref, cols_ref, table_ref, load_sem,
    send_back, recv_back, send_spec, recv_spec, synth, field_ref, flat_ref, lane_ref, bands_ref,
    stack_ref, power_ref, powers_ref, scale_ref, gram_ref, root_ref, up_ref, down_ref,
    edge_up, edge_up_in, edge_down, edge_down_in, rim_up, rim_up_in, rim_down, rim_down_in,
    piece_send, piece_recv, edge_send, edge_recv, stack_send, stack_recv,
    power_send, power_recv, gram_send, gram_recv,
):
    parts = facets * halves
    channels, own, columns = next_ref.shape
    height = base_ref.shape[1]
    lanes = send_back.shape[3]
    tiles = columns // 128
    counts = [len(of_phase) for of_phase in sizes]
    firsts = [[sum(of_phase[:i]) for i in range(len(of_phase))] for of_phase in sizes]
    half = lax.axis_index("sub")
    me = lax.axis_index("facet") * halves + half
    chan = lax.axis_index("chan")

    def place(peer):
        return {"facet": lax.div(peer, halves), "sub": lax.rem(peer, halves)}

    def remote(source, target, sent, received, device):
        return pltpu.make_async_remote_copy(
            src_ref=source, dst_ref=target, send_sem=sent, recv_sem=received,
            device_id=device, device_id_type=MESH,
        )

    def piece_copy(phase, chunk, d):
        source, target = ((send_back, recv_back), (send_spec, recv_spec))[phase]
        peer = lax.rem(me + d, parts)
        span = pl.ds(firsts[phase][chunk], sizes[phase][chunk])
        return remote(
            source.at[peer, span], target.at[me, span],
            piece_send.at[phase, chunk, d - 1], piece_recv.at[phase, chunk, d - 1], place(peer),
        )

    def chan_copy(buffer, sent, received, d):
        return remote(
            buffer.at[chan], buffer.at[chan], sent.at[d - 1], received.at[d - 1],
            {"chan": lax.rem(chan + d, chans)},
        )

    def gram_copy(d):
        return remote(
            gram_ref.at[half], gram_ref.at[half], gram_send.at[d - 1], gram_recv.at[d - 1],
            {"sub": lax.rem(half + d, halves)},
        )

    def each(low, high, action):
        def run(i, carry):
            action(i)
            return carry

        lax.fori_loop(low, high, run, 0)

    def rim_copy(slot, source, target, up):
        peer = lax.rem(me + (parts - 1 if up else 1), parts)
        return remote(source, target, edge_send.at[slot], edge_recv.at[slot], place(peer))

    def neighbours(slot, up_source, up_target, down_source, down_target, action):
        @pl.when(me > 0)
        def _():
            action(rim_copy(slot, up_source, up_target, True), True)

        @pl.when(me < parts - 1)
        def _():
            action(rim_copy(slot + 1, down_source, down_target, False), False)

    def started(copy, up):
        copy.start()

    def arrived(slot, up_source, up_target, down_source, down_target):
        @pl.when(me < parts - 1)
        def _():
            rim_copy(slot, up_source, up_target, True).wait_recv()

        @pl.when(me > 0)
        def _():
            rim_copy(slot + 1, down_source, down_target, False).wait_recv()

    def left(copy, up):
        copy.wait_send()

    early, late = pl.ds(0, sizes[0][0]), pl.ds(sizes[0][0], channels - sizes[0][0])
    loads = [
        pltpu.make_async_copy(source, target, load_sem.at[i])
        for i, (source, target) in enumerate(
            (
                (rows_hbm, rows_ref), (base_hbm, base_ref),
                (dual_hbm.at[early], data_ref.at[early]), (dual_hbm.at[late], data_ref.at[late]),
                (wave_hbm, wavelet_ref), (cols_hbm, cols_ref), (image_hbm, next_ref),
                (nuclear_hbm, mixed_ref), (obs_hbm, obs_ref),
            )
        )
    ]
    for load in loads[:3]:
        load.start()

    for buffer in (edge_up_in, edge_down_in, rim_up_in, rim_down_in):
        buffer[...] = jnp.zeros_like(buffer)

    barrier = pltpu.get_barrier_semaphore()
    each(
        1, parts,
        lambda d: pl.semaphore_signal(
            barrier, inc=1, device_id=place(lax.rem(me + d, parts)), device_id_type=MESH
        ),
    )
    each(
        1, chans,
        lambda d: pl.semaphore_signal(
            barrier, inc=1, device_id={"chan": lax.rem(chan + d, chans)}, device_id_type=MESH
        ),
    )
    loads[3].start()

    def spread(c):
        tables = sample_tables(rows_ref[c], base_ref[...])
        table_ref[c] = tables
        real = data_ref[c, 0].astype(LOW)
        imag = data_ref[c, 1].astype(LOW)
        pair = jnp.concatenate(
            [jnp.concatenate([real, -imag], 1), jnp.concatenate([imag, real], 1)], 0
        )
        total = contract(tables, pair, 1, 1)
        send_back[:, c] = total.astype(LOW).reshape(parts, own, lanes)

    def by_group(phase, chunk, action):
        first, count = firsts[phase][chunk], sizes[phase][chunk]
        pair = math.gcd(count, 4)

        def run(g):
            for i in range(pair):
                action(first + g * pair + i)

        each(0, count // pair, run)

    def send_pieces(phase, chunk):
        each(1, parts, lambda d: piece_copy(phase, chunk, d).start())

    def wave(c):
        colled = []
        for row_band in range(2):
            first = wavelet_ref[c, 2 * row_band].astype(FULL)
            second = wavelet_ref[c, 2 * row_band + 1].astype(FULL)
            colled.append(
                sum(
                    shifted(FILTERS[0][k] * first + FILTERS[1][k] * second, 1 - k, 1)
                    for k in range(4)
                )
            )
        tapped = [FILTERS[0][k] * colled[0] + FILTERS[1][k] * colled[1] for k in range(4)]
        synth[c] = sum(shifted(tapped[k], 1 - k, 0) for k in range(4))
        up_ref[0, pl.ds(c, 1), :] = tapped[0][0:1]
        below = tapped[2] + pltpu.roll(tapped[3], 1, 0)
        down_ref[0, pl.ds(c, 1), :] = below[own - 1 : own]
        down_ref[1, pl.ds(c, 1), :] = tapped[3][own - 1 : own]

    edges = (0, edge_up, edge_up_in, edge_down, edge_down_in)
    for load in loads[:3]:
        load.wait()
    for chunk in range(counts[0]):
        if chunk == 1:
            loads[3].wait()
        by_group(0, chunk, spread)
        if chunk == 0:
            pl.semaphore_wait(barrier, parts + chans - 2)
        send_pieces(0, chunk)
        if chunk == 0:
            for load in loads[4:]:
                load.start()
        if chunk == min(1, counts[0] - 1):
            loads[4].wait()
            each(0, channels, wave)
            edge_up[...] = up_ref[0].astype(LOW)
            edge_down[...] = down_ref[...].astype(LOW)
            neighbours(*edges, started)
    each(0, channels, lambda c: recv_back.__setitem__((me, c), send_back[me, c]))

    for load in loads[5:8]:
        load.wait()
    arrived(*edges)
    up_ref[0] = edge_up_in[...].astype(FULL)
    down_ref[...] = edge_down_in[...].astype(FULL)
    row = lax.broadcasted_iota(jnp.int32, (own, columns), 0)
    group = 2 if lanes == 128 and parts % 2 == 0 else 1

    for chunk in range(counts[0]):
        each(1, parts, lambda d: piece_copy(0, chunk, d).wait_recv())
        first, block = firsts[0][chunk], sizes[0][chunk]
        span = pl.ds(first, block)
        back = 0.0
        for p in range(0, parts, group):
            pieces = [recv_back[p + i, span].reshape(block * own, lanes) for i in range(group)]
            base = cols_ref[p : p + group].reshape(group * lanes, columns)
            back = back + contract(jnp.concatenate(pieces, 1), base, 1, 0)
        flat_ref[pl.ds(first * own, block * own), :] = back

        def update(c):
            start = pl.multiple_of(c * own, own)
            total = flat_ref[pl.ds(start, own), :] + synth[c]
            total += jnp.where(row == own - 1, up_ref[0, pl.ds(c, 1), :], 0.0)
            total += jnp.where(row == 0, down_ref[0, pl.ds(c, 1), :], 0.0)
            total += jnp.where(row == 1, down_ref[1, pl.ds(c, 1), :], 0.0)
            image = next_ref[c]
            nuclear = mixed_ref[c]
            image_next = jnp.maximum(image - 0.5 * (total + nuclear), 0.0)
            field = 2.0 * image_next - image
            next_ref[c] = image_next
            field_ref[c] = field
            stacked = nuclear + field
            for j in range(tiles):
                lane_ref[j, pl.ds(start, own), :] = stacked[:, j * 128 : (j + 1) * 128]
            up_ref[0, pl.ds(c, 1), :] = field[0:1]
            up_ref[1, pl.ds(c, 1), :] = field[1:2]
            down_ref[0, pl.ds(c, 1), :] = field[own - 1 : own]

        each(first, first + block, update)
        low = field_ref[span].reshape(block * own, columns).astype(LOW)
        for p in range(0, parts, group):
            base = cols_ref[p : p + group].reshape(group * lanes, columns)
            spec = contract(low, base, 1, 1).astype(LOW)
            for i in range(group):
                send_spec[p + i, span] = spec[:, i * lanes : (i + 1) * lanes].reshape(
                    block, own, lanes
                )
        if chunk == 0:
            send_pieces(1, chunk)

    rims = (2, rim_up, rim_up_in, rim_down, rim_down_in)
    rim_up[...] = up_ref[...].astype(LOW)
    rim_down[...] = down_ref[0].astype(LOW)
    neighbours(*rims, started)
    for chunk in range(1, counts[1]):
        send_pieces(1, chunk)

    for r in range(own):
        for j in range(tiles):
            picked = lane_ref[j, pl.ds(r, channels, stride=own), :]
            stack_ref[chan, r, :, j * 128 : (j + 1) * 128] = picked.astype(LOW)
    each(1, chans, lambda d: chan_copy(stack_ref, stack_send, stack_recv, d).start())
    each(0, channels, lambda c: recv_spec.__setitem__((me, c), send_spec[me, c]))
    power_ref[...] = jnp.zeros_like(power_ref)
    arrived(*rims)
    up_ref[...] = rim_up_in[...].astype(FULL)
    down_ref[0] = rim_down_in[...].astype(FULL)

    def analyse(c):
        field = field_ref[c]
        above = down_ref[0, pl.ds(c, 1), :]
        below = up_ref[0, pl.ds(c, 1), :]
        beyond = up_ref[1, pl.ds(c, 1), :]
        moved = [
            jnp.where(row == 0, above, pltpu.roll(field, 1, 0)),
            field,
            jnp.where(row == own - 1, below, pltpu.roll(field, own - 1, 0)),
            jnp.where(
                row == own - 1, beyond,
                jnp.where(row == own - 2, below, pltpu.roll(field, own - 2, 0)),
            ),
        ]
        for row_band in range(2):
            rowed = sum(FILTERS[row_band][k] * moved[k] for k in range(4))
            spots = [shifted(rowed, k - 1, 1) for k in range(4)]
            for col_band in range(2):
                band = 2 * row_band + col_band
                value = sum((0.5 * FILTERS[col_band][k]) * spots[k] for k in range(4))
                value += wavelet_ref[c, band].astype(FULL)
                bands_ref[c, band] = value
                power_ref[band] += value * value

    each(0, channels, analyse)
    powers_ref[chan] = power_ref[...].astype(LOW)
    each(1, chans, lambda d: chan_copy(powers_ref, power_send, power_recv, d).start())

    def sample(c):
        spec = recv_spec[:, c].reshape(height, lanes)
        dual, seen = (data_ref[c, 0], data_ref[c, 1]), (obs_ref[c, 0], obs_ref[c, 1])
        data_ref[c, 0], data_ref[c, 1] = data_step(spec, table_ref[c], dual, seen)

    def finish(chunk):
        each(1, parts, lambda d: piece_copy(1, chunk, d).wait_recv())
        by_group(1, chunk, sample)

    loads[8].wait()
    ends = [first + count for first, count in zip(firsts[1], sizes[1])]
    soon = sum(8 * end <= 3 * channels for end in ends)
    later = sum(3 * end <= 2 * channels for end in ends)
    for chunk in range(soon):
        finish(chunk)

    def stacked_rows(r):
        if channels % 16 == 0:
            return jnp.concatenate([stack_ref[n, r] for n in range(chans)], 0)
        return jnp.concatenate([stack_ref[n, r].astype(FULL) for n in range(chans)], 0).astype(LOW)

    each(1, chans, lambda d: chan_copy(stack_ref, stack_send, stack_recv, d).wait_recv())
    total = chans * channels
    gram_ref[half] = jnp.zeros((total, total), FULL)

    def gather(g):
        part = 0.0
        for i in range(4):
            rows = stacked_rows(g * 4 + i)
            part = part + contract(rows, rows, 1, 1)
        gram_ref[half] += part

    each(0, own // 4, gather)
    each(1, halves, lambda d: gram_copy(d).start())

    each(1, chans, lambda d: chan_copy(powers_ref, power_send, power_recv, d).wait_recv())
    limit = 0.6 * math.sqrt(CH)
    for band in range(4):
        power = sum(powers_ref[n, band].astype(FULL) for n in range(chans))
        scale_ref[band] = 1.0 / jnp.maximum(1.0, jnp.sqrt(power) / limit)

    def shrink(c):
        wavelet_ref[c] = (bands_ref[c] * scale_ref[...]).astype(LOW)

    each(0, channels, shrink)
    for chunk in range(soon, later):
        finish(chunk)

    each(1, halves, lambda d: gram_copy(d).wait_recv())
    gram = sum(gram_ref[h] for h in range(halves))
    diagonal = lax.broadcasted_iota(jnp.int32, (total, total), 0) == lax.broadcasted_iota(
        jnp.int32, (total, total), 1
    )
    trace_sum = jnp.sum(jnp.where(diagonal, gram, 0.0), keepdims=True)
    eye = jnp.where(diagonal, 1.0, 0.0)
    approx = (2.0 / trace_sum) * gram
    root = eye

    def exact(left_side, right_side):
        return jnp.dot(left_side, right_side, precision=HIGH, preferred_element_type=FULL)

    for turn in range(NS_STEPS):
        newton = 1.5 * eye - 0.5 * exact(root, approx)
        approx = exact(approx, newton)
        root = exact(newton, root)
    factor = jnp.sqrt(2.0 * (own * columns * halves) / trace_sum)
    root_ref[...] = root
    mine = root_ref[pl.ds(pl.multiple_of(chan * channels, channels), channels), :].astype(LOW)
    for r in range(own):
        mixed = jnp.dot(mine, stacked_rows(r), preferred_element_type=FULL)
        mixed = factor * mixed
        for j in range(tiles):
            lane_ref[j, pl.ds(r, channels, stride=own), :] = mixed[:, j * 128 : (j + 1) * 128]

    def place_mixed(c):
        start = pl.multiple_of(c * own, own)
        for j in range(tiles):
            mixed_ref[c, :, j * 128 : (j + 1) * 128] = lane_ref[j, pl.ds(start, own), :]

    each(0, channels, place_mixed)

    tail = pl.ds(firsts[1][-1], sizes[1][-1])
    last_table[...] = table_ref[tail]
    last_obs[...] = obs_ref[tail]
    for chunk in range(later, counts[1] - 1):
        finish(chunk)
    each(1, parts, lambda d: piece_copy(1, counts[1] - 1, d).wait_recv())
    last_spec[...] = recv_spec[:, tail]

    for phase in range(2):
        for chunk in range(counts[phase]):
            each(1, parts, lambda d: piece_copy(phase, chunk, d).wait_send())
    neighbours(*edges, left)
    neighbours(*rims, left)
    each(1, chans, lambda d: chan_copy(stack_ref, stack_send, stack_recv, d).wait_send())
    each(1, chans, lambda d: chan_copy(powers_ref, power_send, power_recv, d).wait_send())
    each(1, halves, lambda d: gram_copy(d).wait_send())


def write_kernel(
    next_ref, mixed_ref, wavelet_ref, data_ref, spec_ref, table_ref, obs_ref,
    next_hbm, mixed_hbm, wavelet_hbm, data_hbm, done_ref, sem,
):
    parts, count, own, lanes = spec_ref.shape
    first = data_ref.shape[0] - count
    early, late = pl.ds(0, first), pl.ds(first, count)
    copies = [
        pltpu.make_async_copy(source, target, sem.at[i])
        for i, (source, target) in enumerate(
            (
                (next_ref, next_hbm), (mixed_ref, mixed_hbm), (wavelet_ref, wavelet_hbm),
                (data_ref.at[early], data_hbm.at[early]), (done_ref, data_hbm.at[late]),
            )
        )
    ]
    for copy in copies[:4]:
        copy.start()
    for i in range(count):
        c = first + i
        spec = spec_ref[:, i].reshape(parts * own, lanes)
        dual, seen = (data_ref[c, 0], data_ref[c, 1]), (obs_ref[i, 0], obs_ref[i, 1])
        done_ref[i, 0], done_ref[i, 1] = data_step(spec, table_ref[i], dual, seen)
    copies[4].start()
    for copy in copies:
        copy.wait()


def shards(image, dual_nuclear, dual_wavelet, dual_data, observed, sample_rows):
    channels, own, columns = image.shape
    facets = lax.axis_size("facet")
    halves = lax.axis_size("sub")
    chans = lax.axis_size("chan")
    parts = facets * halves
    height = own * parts
    lanes = 2 * dual_data.shape[2]
    sizes = chunk_sizes(channels)
    chunks = max(len(of_phase) for of_phase in sizes)
    total = channels * chans
    bands = dual_wavelet.shape[1]
    here = pl.BlockSpec(memory_space=pltpu.VMEM)
    away = pl.BlockSpec(memory_space=pltpu.HBM)
    rows = sample_rows.reshape(channels, 1, -1)
    base = row_base(height)
    cols = col_base(columns, parts)
    piece = pltpu.VMEM((parts, channels, own, lanes), LOW)
    plane = pltpu.VMEM((channels, columns), LOW)
    planes = pltpu.VMEM((2, channels, columns), LOW)
    wide = pltpu.VMEM((2, channels, columns), FULL)
    dma = pltpu.SemaphoreType.DMA
    last = sizes[1][-1]
    table = (height, 2 * dual_data.shape[3])
    outs = (
        (image.shape, FULL), (image.shape, FULL), (dual_wavelet.shape, LOW), (dual_data.shape, FULL),
    )
    handed = (
        ((parts, last, own, lanes), LOW), ((last, *table), LOW), ((last, *observed.shape[1:]), FULL),
    )
    operands = [
        pltpu.with_memory_space_constraint(x, pltpu.HBM)
        for x in (rows, image, dual_nuclear, dual_wavelet, dual_data, observed, base, cols)
    ]
    results = pl.pallas_call(
        functools.partial(step_kernel, facets, halves, chans, sizes),
        name="step",
        out_shape=tuple(pltpu.VMEM(*out) for out in outs + handed),
        in_specs=[away] * 8,
        out_specs=[here] * 7,
        scratch_shapes=[
            pltpu.VMEM(rows.shape, jnp.int32), pltpu.VMEM(observed.shape, FULL),
            pltpu.VMEM(base.shape, LOW), pltpu.VMEM(cols.shape, LOW),
            pltpu.VMEM((channels, *table), LOW), dma((9,)),
            piece, piece, piece, piece,
            pltpu.VMEM(image.shape, FULL),
            pltpu.VMEM(image.shape, FULL),
            pltpu.VMEM((channels * own, columns), FULL),
            pltpu.VMEM((columns // 128, channels * own, 128), FULL),
            pltpu.VMEM(dual_wavelet.shape, FULL),
            pltpu.VMEM((chans, own, channels, columns), LOW),
            pltpu.VMEM((bands, own, columns), FULL),
            pltpu.VMEM((chans, bands, own, columns), LOW),
            pltpu.VMEM((bands, own, columns), FULL),
            pltpu.VMEM((halves, total, total), FULL),
            pltpu.VMEM((total, total), FULL),
            wide, wide,
            plane, plane, planes, planes, planes, planes, plane, plane,
            dma((2, chunks, parts - 1)), dma((2, chunks, parts - 1)),
            dma((4,)), dma((4,)),
            dma((chans - 1,)), dma((chans - 1,)),
            dma((chans - 1,)), dma((chans - 1,)),
            dma((halves - 1,)), dma((halves - 1,)),
        ],
        compiler_params=pltpu.CompilerParams(
            collective_id=0, has_side_effects=True, vmem_limit_bytes=44000000
        ),
    )(*operands)
    return pl.pallas_call(
        write_kernel,
        name="write",
        out_shape=tuple(jax.ShapeDtypeStruct(*out) for out in outs),
        in_specs=[here] * 7,
        out_specs=[away] * 4,
        scratch_shapes=[pltpu.VMEM((last, *observed.shape[1:]), FULL), dma((5,))],
        compiler_params=pltpu.CompilerParams(vmem_limit_bytes=3000000),
    )(*(pltpu.with_memory_space_constraint(x, pltpu.VMEM) for x in results))


def solution(mesh):
    placed = (
        P(("cube", "chan"), ("facet", "sub"), None),
        P(("cube", "chan"), ("facet", "sub"), None),
        P(("cube", "chan"), None, ("facet", "sub"), None),
        P(("cube", "chan"), None, ("facet", "sub"), None),
        P(("cube", "chan"), None, ("facet", "sub"), None),
        P(("cube", "chan"), None),
    )
    return jax.shard_map(
        shards,
        mesh=mesh,
        in_specs=placed,
        out_specs=(
            P(("cube", "chan"), ("facet", "sub"), None),
            P(("cube", "chan"), ("facet", "sub"), None),
            P(("cube", "chan"), None, ("facet", "sub"), None),
            P(("cube", "chan"), None, ("facet", "sub"), None),
        ),
        check_vma=False,
    )
```

```python
import functools
import math

import jax
import jax.numpy as jnp
import numpy as np
from jax import lax
from jax.experimental import pallas as pl
from jax.experimental.pallas import tpu as pltpu
from jax.sharding import PartitionSpec as P

CH = 64
NS_STEPS = 6


LOWPASS = [0.48296291314453416, 0.8365163037378079, 0.2241438680420134, -0.12940952255126037]
FILTERS = [
    [value / math.sqrt(2.0) for value in LOWPASS],
    [(-1.0) ** index * LOWPASS[3 - index] / math.sqrt(2.0) for index in range(4)],
]
HIGH = lax.Precision.HIGHEST
LOW = jnp.bfloat16
MESH = pl.DeviceIdType.MESH
FULL = jnp.float32


def phase_base(period):
    places = np.arange(period)
    angles = np.float32(2.0 * math.pi / period) * (np.outer(places, places) % period).astype(np.float32)
    norm = np.float32(1.0 / math.sqrt(period))
    return np.cos(angles) * norm, np.sin(angles) * norm


def row_base(height):
    return jnp.asarray(np.concatenate(phase_base(height), 0).astype(LOW))


def col_base(columns, parts):
    cosine, sine = (t.reshape(parts, columns // parts, columns) for t in phase_base(columns))
    return jnp.asarray(np.concatenate([cosine, -sine], 1).astype(LOW))


def sample_tables(rows, base):
    height, samples = base.shape[1], rows.shape[1]
    hot = lax.broadcasted_iota(jnp.int32, (height, samples), 0) == rows
    hot = jnp.where(hot, 1.0, 0.0).astype(LOW)
    both = jnp.dot(base, hot, preferred_element_type=jnp.float32).astype(LOW)
    return jnp.concatenate([both[:height], both[height:]], 1)


def contract(left, right, left_dim, right_dim):
    return lax.dot_general(
        left, right, (((left_dim,), (right_dim,)), ((), ())), preferred_element_type=jnp.float32
    )


def data_step(spec, tables, dual, seen):
    width, samples = dual[0].shape
    both = contract(spec, tables, 0, 0)
    real = both[:width, :samples] + both[width:, samples:]
    imag = both[width:, :samples] - both[:width, samples:]
    return [(d + 0.5 * (v - o)) / 1.5 for d, v, o in zip(dual, (real, imag), seen)]


def shifted(values, offset, axis):
    length = values.shape[axis]
    if offset == 0:
        return values
    place = lax.broadcasted_iota(jnp.int32, values.shape, axis) + offset
    moved = pltpu.roll(values, (-offset) % length, axis)
    return jnp.where((place >= 0) & (place < length), moved, 0.0)


def chunk_sizes(channels):
    if channels % 16 == 0:
        share = channels // 16
        return ([2 * share, 7 * share, 7 * share],) * 2
    unit = math.gcd(channels, 4)
    return ([unit] * (channels // unit),) * 2


def step_kernel(
    facets, halves, chans, sizes,
    rows_hbm, image_hbm, nuclear_hbm, wave_hbm, dual_hbm, obs_hbm, base_hbm, cols_hbm,
    next_ref, mixed_ref, wavelet_ref, data_ref, last_spec, last_table, last_obs,
    rows_ref, obs_ref, base_ref, cols_ref, table_ref, load_sem,
    send_back, recv_back, send_spec, recv_spec, synth, field_ref, flat_ref, lane_ref, bands_ref,
    stack_ref, power_ref, powers_ref, scale_ref, gram_ref, root_ref, up_ref, down_ref,
    edge_up, edge_up_in, edge_down, edge_down_in, rim_up, rim_up_in, rim_down, rim_down_in,
    piece_send, piece_recv, edge_send, edge_recv, stack_send, stack_recv,
    power_send, power_recv, gram_send, gram_recv,
):
    parts = facets * halves
    channels, own, columns = next_ref.shape
    height = base_ref.shape[1]
    lanes = send_back.shape[3]
    tiles = columns // 128
    counts = [len(of_phase) for of_phase in sizes]
    firsts = [[sum(of_phase[:i]) for i in range(len(of_phase))] for of_phase in sizes]
    half = lax.axis_index("sub")
    me = lax.axis_index("facet") * halves + half
    chan = lax.axis_index("chan")

    def place(peer):
        return {"facet": lax.div(peer, halves), "sub": lax.rem(peer, halves)}

    def remote(source, target, sent, received, device):
        return pltpu.make_async_remote_copy(
            src_ref=source, dst_ref=target, send_sem=sent, recv_sem=received,
            device_id=device, device_id_type=MESH,
        )

    def piece_copy(phase, chunk, d):
        source, target = ((send_back, recv_back), (send_spec, recv_spec))[phase]
        peer = lax.rem(me + d, parts)
        span = pl.ds(firsts[phase][chunk], sizes[phase][chunk])
        return remote(
            source.at[peer, span], target.at[me, span],
            piece_send.at[phase, chunk, d - 1], piece_recv.at[phase, chunk, d - 1], place(peer),
        )

    def chan_copy(buffer, sent, received, d):
        return remote(
            buffer.at[chan], buffer.at[chan], sent.at[d - 1], received.at[d - 1],
            {"chan": lax.rem(chan + d, chans)},
        )

    def gram_copy(d):
        return remote(
            gram_ref.at[half], gram_ref.at[half], gram_send.at[d - 1], gram_recv.at[d - 1],
            {"sub": lax.rem(half + d, halves)},
        )

    def each(low, high, action):
        def run(i, carry):
            action(i)
            return carry

        lax.fori_loop(low, high, run, 0)

    def rim_copy(slot, source, target, up):
        peer = lax.rem(me + (parts - 1 if up else 1), parts)
        return remote(source, target, edge_send.at[slot], edge_recv.at[slot], place(peer))

    def neighbours(slot, up_source, up_target, down_source, down_target, action):
        @pl.when(me > 0)
        def _():
            action(rim_copy(slot, up_source, up_target, True), True)

        @pl.when(me < parts - 1)
        def _():
            action(rim_copy(slot + 1, down_source, down_target, False), False)

    def started(copy, up):
        copy.start()

    def arrived(slot, up_source, up_target, down_source, down_target):
        @pl.when(me < parts - 1)
        def _():
            rim_copy(slot, up_source, up_target, True).wait_recv()

        @pl.when(me > 0)
        def _():
            rim_copy(slot + 1, down_source, down_target, False).wait_recv()

    def left(copy, up):
        copy.wait_send()

    early, late = pl.ds(0, sizes[0][0]), pl.ds(sizes[0][0], channels - sizes[0][0])
    loads = [
        pltpu.make_async_copy(source, target, load_sem.at[i])
        for i, (source, target) in enumerate(
            (
                (rows_hbm, rows_ref), (base_hbm, base_ref),
                (dual_hbm.at[early], data_ref.at[early]), (dual_hbm.at[late], data_ref.at[late]),
                (wave_hbm, wavelet_ref), (cols_hbm, cols_ref), (image_hbm, next_ref),
                (nuclear_hbm, mixed_ref), (obs_hbm, obs_ref),
            )
        )
    ]
    for buffer in (edge_up_in, edge_down_in, rim_up_in, rim_down_in):
        buffer[...] = jnp.zeros_like(buffer)

    barrier = pltpu.get_barrier_semaphore()
    each(
        1, parts,
        lambda d: pl.semaphore_signal(
            barrier, inc=1, device_id=place(lax.rem(me + d, parts)), device_id_type=MESH
        ),
    )
    each(
        1, chans,
        lambda d: pl.semaphore_signal(
            barrier, inc=1, device_id={"chan": lax.rem(chan + d, chans)}, device_id_type=MESH
        ),
    )
    for load in loads[:4]:
        load.start()

    def spread(c):
        tables = sample_tables(rows_ref[c], base_ref[...])
        table_ref[c] = tables
        real = data_ref[c, 0].astype(LOW)
        imag = data_ref[c, 1].astype(LOW)
        pair = jnp.concatenate(
            [jnp.concatenate([real, -imag], 1), jnp.concatenate([imag, real], 1)], 0
        )
        total = contract(tables, pair, 1, 1)
        send_back[:, c] = total.astype(LOW).reshape(parts, own, lanes)

    def by_group(phase, chunk, action):
        first, count = firsts[phase][chunk], sizes[phase][chunk]
        pair = math.gcd(count, 4)

        def run(g):
            for i in range(pair):
                action(first + g * pair + i)

        each(0, count // pair, run)

    def send_pieces(phase, chunk):
        each(1, parts, lambda d: piece_copy(phase, chunk, d).start())

    def wave(c):
        colled = []
        for row_band in range(2):
            first = wavelet_ref[c, 2 * row_band].astype(FULL)
            second = wavelet_ref[c, 2 * row_band + 1].astype(FULL)
            colled.append(
                sum(
                    shifted(FILTERS[0][k] * first + FILTERS[1][k] * second, 1 - k, 1)
                    for k in range(4)
                )
            )
        tapped = [FILTERS[0][k] * colled[0] + FILTERS[1][k] * colled[1] for k in range(4)]
        synth[c] = sum(shifted(tapped[k], 1 - k, 0) for k in range(4))
        up_ref[0, pl.ds(c, 1), :] = tapped[0][0:1]
        below = tapped[2] + pltpu.roll(tapped[3], 1, 0)
        down_ref[0, pl.ds(c, 1), :] = below[own - 1 : own]
        down_ref[1, pl.ds(c, 1), :] = tapped[3][own - 1 : own]

    edges = (0, edge_up, edge_up_in, edge_down, edge_down_in)
    for load in loads[:3]:
        load.wait()
    for chunk in range(counts[0]):
        if chunk == 1:
            loads[3].wait()
        by_group(0, chunk, spread)
        if chunk == 0:
            pl.semaphore_wait(barrier, parts + chans - 2)
        send_pieces(0, chunk)
        if chunk == 0:
            for load in loads[4:]:
                load.start()
        if chunk == min(1, counts[0] - 1):
            loads[4].wait()
            each(0, channels, wave)
            edge_up[...] = up_ref[0].astype(LOW)
            edge_down[...] = down_ref[...].astype(LOW)
            neighbours(*edges, started)
    each(0, channels, lambda c: recv_back.__setitem__((me, c), send_back[me, c]))

    for load in loads[5:8]:
        load.wait()
    arrived(*edges)
    up_ref[0] = edge_up_in[...].astype(FULL)
    down_ref[...] = edge_down_in[...].astype(FULL)
    row = lax.broadcasted_iota(jnp.int32, (own, columns), 0)
    group = 2 if lanes == 128 and parts % 2 == 0 else 1

    for chunk in range(counts[0]):
        each(1, parts, lambda d: piece_copy(0, chunk, d).wait_recv())
        first, block = firsts[0][chunk], sizes[0][chunk]
        span = pl.ds(first, block)
        back = 0.0
        for p in range(0, parts, group):
            pieces = [recv_back[p + i, span].reshape(block * own, lanes) for i in range(group)]
            base = cols_ref[p : p + group].reshape(group * lanes, columns)
            back = back + contract(jnp.concatenate(pieces, 1), base, 1, 0)
        flat_ref[pl.ds(first * own, block * own), :] = back

        def update(c):
            start = pl.multiple_of(c * own, own)
            total = flat_ref[pl.ds(start, own), :] + synth[c]
            total += jnp.where(row == own - 1, up_ref[0, pl.ds(c, 1), :], 0.0)
            total += jnp.where(row == 0, down_ref[0, pl.ds(c, 1), :], 0.0)
            total += jnp.where(row == 1, down_ref[1, pl.ds(c, 1), :], 0.0)
            image = next_ref[c]
            nuclear = mixed_ref[c]
            image_next = jnp.maximum(image - 0.5 * (total + nuclear), 0.0)
            field = 2.0 * image_next - image
            next_ref[c] = image_next
            field_ref[c] = field
            stacked = nuclear + field
            for j in range(tiles):
                lane_ref[j, pl.ds(start, own), :] = stacked[:, j * 128 : (j + 1) * 128]
            up_ref[0, pl.ds(c, 1), :] = field[0:1]
            up_ref[1, pl.ds(c, 1), :] = field[1:2]
            down_ref[0, pl.ds(c, 1), :] = field[own - 1 : own]

        each(first, first + block, update)
        low = field_ref[span].reshape(block * own, columns).astype(LOW)
        for p in range(0, parts, group):
            base = cols_ref[p : p + group].reshape(group * lanes, columns)
            spec = contract(low, base, 1, 1).astype(LOW)
            for i in range(group):
                send_spec[p + i, span] = spec[:, i * lanes : (i + 1) * lanes].reshape(
                    block, own, lanes
                )
        if chunk == 0:
            send_pieces(1, chunk)

    rims = (2, rim_up, rim_up_in, rim_down, rim_down_in)
    rim_up[...] = up_ref[...].astype(LOW)
    rim_down[...] = down_ref[0].astype(LOW)
    neighbours(*rims, started)
    for chunk in range(1, counts[1]):
        send_pieces(1, chunk)

    for r in range(own):
        for j in range(tiles):
            picked = lane_ref[j, pl.ds(r, channels, stride=own), :]
            stack_ref[chan, r, :, j * 128 : (j + 1) * 128] = picked.astype(LOW)
    each(1, chans, lambda d: chan_copy(stack_ref, stack_send, stack_recv, d).start())
    each(0, channels, lambda c: recv_spec.__setitem__((me, c), send_spec[me, c]))
    power_ref[...] = jnp.zeros_like(power_ref)
    arrived(*rims)
    up_ref[...] = rim_up_in[...].astype(FULL)
    down_ref[0] = rim_down_in[...].astype(FULL)

    def analyse(c):
        field = field_ref[c]
        above = down_ref[0, pl.ds(c, 1), :]
        below = up_ref[0, pl.ds(c, 1), :]
        beyond = up_ref[1, pl.ds(c, 1), :]
        moved = [
            jnp.where(row == 0, above, pltpu.roll(field, 1, 0)),
            field,
            jnp.where(row == own - 1, below, pltpu.roll(field, own - 1, 0)),
            jnp.where(
                row == own - 1, beyond,
                jnp.where(row == own - 2, below, pltpu.roll(field, own - 2, 0)),
            ),
        ]
        for row_band in range(2):
            rowed = sum(FILTERS[row_band][k] * moved[k] for k in range(4))
            spots = [shifted(rowed, k - 1, 1) for k in range(4)]
            for col_band in range(2):
                band = 2 * row_band + col_band
                value = sum((0.5 * FILTERS[col_band][k]) * spots[k] for k in range(4))
                value += wavelet_ref[c, band].astype(FULL)
                bands_ref[c, band] = value
                power_ref[band] += value * value

    each(0, channels, analyse)
    powers_ref[chan] = power_ref[...].astype(LOW)
    each(1, chans, lambda d: chan_copy(powers_ref, power_send, power_recv, d).start())

    def sample(c):
        spec = recv_spec[:, c].reshape(height, lanes)
        dual, seen = (data_ref[c, 0], data_ref[c, 1]), (obs_ref[c, 0], obs_ref[c, 1])
        data_ref[c, 0], data_ref[c, 1] = data_step(spec, table_ref[c], dual, seen)

    def finish(chunk):
        each(1, parts, lambda d: piece_copy(1, chunk, d).wait_recv())
        by_group(1, chunk, sample)

    loads[8].wait()
    ends = [first + count for first, count in zip(firsts[1], sizes[1])]
    soon = sum(8 * end <= 3 * channels for end in ends)
    later = sum(3 * end <= 2 * channels for end in ends)
    for chunk in range(soon):
        finish(chunk)

    def stacked_rows(r):
        if channels % 16 == 0:
            return jnp.concatenate([stack_ref[n, r] for n in range(chans)], 0)
        return jnp.concatenate([stack_ref[n, r].astype(FULL) for n in range(chans)], 0).astype(LOW)

    each(1, chans, lambda d: chan_copy(stack_ref, stack_send, stack_recv, d).wait_recv())
    total = chans * channels
    gram_ref[half] = jnp.zeros((total, total), FULL)

    def gather(g):
        part = 0.0
        for i in range(4):
            rows = stacked_rows(g * 4 + i)
            part = part + contract(rows, rows, 1, 1)
        gram_ref[half] += part

    each(0, own // 4, gather)
    each(1, halves, lambda d: gram_copy(d).start())

    each(1, chans, lambda d: chan_copy(powers_ref, power_send, power_recv, d).wait_recv())
    limit = 0.6 * math.sqrt(CH)
    for band in range(4):
        power = sum(powers_ref[n, band].astype(FULL) for n in range(chans))
        scale_ref[band] = 1.0 / jnp.maximum(1.0, jnp.sqrt(power) / limit)

    def shrink(c):
        wavelet_ref[c] = (bands_ref[c] * scale_ref[...]).astype(LOW)

    each(0, channels, shrink)
    for chunk in range(soon, later):
        finish(chunk)

    each(1, halves, lambda d: gram_copy(d).wait_recv())
    gram = sum(gram_ref[h] for h in range(halves))
    diagonal = lax.broadcasted_iota(jnp.int32, (total, total), 0) == lax.broadcasted_iota(
        jnp.int32, (total, total), 1
    )
    trace_sum = jnp.sum(jnp.where(diagonal, gram, 0.0), keepdims=True)
    eye = jnp.where(diagonal, 1.0, 0.0)
    approx = (2.0 / trace_sum) * gram
    root = eye

    def exact(left_side, right_side):
        return jnp.dot(left_side, right_side, precision=HIGH, preferred_element_type=FULL)

    for turn in range(NS_STEPS):
        newton = 1.5 * eye - 0.5 * exact(root, approx)
        approx = exact(approx, newton)
        root = exact(newton, root)
    factor = jnp.sqrt(2.0 * (own * columns * halves) / trace_sum)
    root_ref[...] = root
    mine = root_ref[pl.ds(pl.multiple_of(chan * channels, channels), channels), :].astype(LOW)
    for r in range(own):
        mixed = jnp.dot(mine, stacked_rows(r), preferred_element_type=FULL)
        mixed = factor * mixed
        for j in range(tiles):
            lane_ref[j, pl.ds(r, channels, stride=own), :] = mixed[:, j * 128 : (j + 1) * 128]

    def place_mixed(c):
        start = pl.multiple_of(c * own, own)
        for j in range(tiles):
            mixed_ref[c, :, j * 128 : (j + 1) * 128] = lane_ref[j, pl.ds(start, own), :]

    each(0, channels, place_mixed)

    tail = pl.ds(firsts[1][-1], sizes[1][-1])
    last_table[...] = table_ref[tail]
    last_obs[...] = obs_ref[tail]
    for chunk in range(later, counts[1] - 1):
        finish(chunk)
    each(1, parts, lambda d: piece_copy(1, counts[1] - 1, d).wait_recv())
    last_spec[...] = recv_spec[:, tail]

    for phase in range(2):
        for chunk in range(counts[phase]):
            each(1, parts, lambda d: piece_copy(phase, chunk, d).wait_send())
    neighbours(*edges, left)
    neighbours(*rims, left)
    each(1, chans, lambda d: chan_copy(stack_ref, stack_send, stack_recv, d).wait_send())
    each(1, chans, lambda d: chan_copy(powers_ref, power_send, power_recv, d).wait_send())
    each(1, halves, lambda d: gram_copy(d).wait_send())


def write_kernel(
    next_ref, mixed_ref, wavelet_ref, data_ref, spec_ref, table_ref, obs_ref,
    next_hbm, mixed_hbm, wavelet_hbm, data_hbm, done_ref, sem,
):
    parts, count, own, lanes = spec_ref.shape
    first = data_ref.shape[0] - count
    early, late = pl.ds(0, first), pl.ds(first, count)
    copies = [
        pltpu.make_async_copy(source, target, sem.at[i])
        for i, (source, target) in enumerate(
            (
                (next_ref, next_hbm), (mixed_ref, mixed_hbm), (wavelet_ref, wavelet_hbm),
                (data_ref.at[early], data_hbm.at[early]), (done_ref, data_hbm.at[late]),
            )
        )
    ]
    for copy in copies[:4]:
        copy.start()
    for i in range(count):
        c = first + i
        spec = spec_ref[:, i].reshape(parts * own, lanes)
        dual, seen = (data_ref[c, 0], data_ref[c, 1]), (obs_ref[i, 0], obs_ref[i, 1])
        done_ref[i, 0], done_ref[i, 1] = data_step(spec, table_ref[i], dual, seen)
    copies[4].start()
    for copy in copies:
        copy.wait()


def shards(image, dual_nuclear, dual_wavelet, dual_data, observed, sample_rows):
    channels, own, columns = image.shape
    facets = lax.axis_size("facet")
    halves = lax.axis_size("sub")
    chans = lax.axis_size("chan")
    parts = facets * halves
    height = own * parts
    lanes = 2 * dual_data.shape[2]
    sizes = chunk_sizes(channels)
    chunks = max(len(of_phase) for of_phase in sizes)
    total = channels * chans
    bands = dual_wavelet.shape[1]
    here = pl.BlockSpec(memory_space=pltpu.VMEM)
    away = pl.BlockSpec(memory_space=pltpu.HBM)
    rows = sample_rows.reshape(channels, 1, -1)
    base = row_base(height)
    cols = col_base(columns, parts)
    piece = pltpu.VMEM((parts, channels, own, lanes), LOW)
    plane = pltpu.VMEM((channels, columns), LOW)
    planes = pltpu.VMEM((2, channels, columns), LOW)
    wide = pltpu.VMEM((2, channels, columns), FULL)
    dma = pltpu.SemaphoreType.DMA
    last = sizes[1][-1]
    table = (height, 2 * dual_data.shape[3])
    outs = (
        (image.shape, FULL), (image.shape, FULL), (dual_wavelet.shape, LOW), (dual_data.shape, FULL),
    )
    handed = (
        ((parts, last, own, lanes), LOW), ((last, *table), LOW), ((last, *observed.shape[1:]), FULL),
    )
    operands = [
        pltpu.with_memory_space_constraint(x, pltpu.HBM)
        for x in (rows, image, dual_nuclear, dual_wavelet, dual_data, observed, base, cols)
    ]
    results = pl.pallas_call(
        functools.partial(step_kernel, facets, halves, chans, sizes),
        name="step",
        out_shape=tuple(pltpu.VMEM(*out) for out in outs + handed),
        in_specs=[away] * 8,
        out_specs=[here] * 7,
        scratch_shapes=[
            pltpu.VMEM(rows.shape, jnp.int32), pltpu.VMEM(observed.shape, FULL),
            pltpu.VMEM(base.shape, LOW), pltpu.VMEM(cols.shape, LOW),
            pltpu.VMEM((channels, *table), LOW), dma((9,)),
            piece, piece, piece, piece,
            pltpu.VMEM(image.shape, FULL),
            pltpu.VMEM(image.shape, FULL),
            pltpu.VMEM((channels * own, columns), FULL),
            pltpu.VMEM((columns // 128, channels * own, 128), FULL),
            pltpu.VMEM(dual_wavelet.shape, FULL),
            pltpu.VMEM((chans, own, channels, columns), LOW),
            pltpu.VMEM((bands, own, columns), FULL),
            pltpu.VMEM((chans, bands, own, columns), LOW),
            pltpu.VMEM((bands, own, columns), FULL),
            pltpu.VMEM((halves, total, total), FULL),
            pltpu.VMEM((total, total), FULL),
            wide, wide,
            plane, plane, planes, planes, planes, planes, plane, plane,
            dma((2, chunks, parts - 1)), dma((2, chunks, parts - 1)),
            dma((4,)), dma((4,)),
            dma((chans - 1,)), dma((chans - 1,)),
            dma((chans - 1,)), dma((chans - 1,)),
            dma((halves - 1,)), dma((halves - 1,)),
        ],
        compiler_params=pltpu.CompilerParams(
            collective_id=0, has_side_effects=True, vmem_limit_bytes=44000000
        ),
    )(*operands)
    return pl.pallas_call(
        write_kernel,
        name="write",
        out_shape=tuple(jax.ShapeDtypeStruct(*out) for out in outs),
        in_specs=[here] * 7,
        out_specs=[away] * 4,
        scratch_shapes=[pltpu.VMEM((last, *observed.shape[1:]), FULL), dma((5,))],
        compiler_params=pltpu.CompilerParams(vmem_limit_bytes=3000000),
    )(*(pltpu.with_memory_space_constraint(x, pltpu.VMEM) for x in results))


def solution(mesh):
    placed = (
        P(("cube", "chan"), ("facet", "sub"), None),
        P(("cube", "chan"), ("facet", "sub"), None),
        P(("cube", "chan"), None, ("facet", "sub"), None),
        P(("cube", "chan"), None, ("facet", "sub"), None),
        P(("cube", "chan"), None, ("facet", "sub"), None),
        P(("cube", "chan"), None),
    )
    return jax.shard_map(
        shards,
        mesh=mesh,
        in_specs=placed,
        out_specs=(
            P(("cube", "chan"), ("facet", "sub"), None),
            P(("cube", "chan"), ("facet", "sub"), None),
            P(("cube", "chan"), None, ("facet", "sub"), None),
            P(("cube", "chan"), None, ("facet", "sub"), None),
        ),
        check_vma=False,
    )
```
